128 devices in a mesh: space: 16 (over z_hi, x, core), band: 8 (over z_lo, y).
Axes of the slice: x: 4, y: 4, z: 4 (z_hi: 2, z_lo: 2; z = z_hi * 2 + z_lo), core: 2. Of those that a mesh axis runs over, the one named last changes fastest.
Arguments:
- blocks: float32 [2, 32, 64, 6144], P(None, 'band', 'space'), may hold values from -304 to 304
- later: float32 [256, 64, 6144], P('band', 'space'), may hold values from -304 to 304
- potential: float32 [64, 6144], P('space'), may hold values from -1.5 to 1.5
Outputs:
- h_block: float32 [2, 32, 64, 6144], P(None, 'band', 'space')
- h_later: float32 [256, 64, 6144], P('band', 'space')
The draws below stay inside these ranges and needn't reach their ends.
All inputs are finite; a program needn't handle non-finite values.
Results may differ from the reference program's by a relative error of at most 0.00009.
Values sent between devices are 32-bit elements; how exact they have to be, the bound alone decides.
A program may use at most 128 MiB of HBM per device.

```python
import jax
import jax.numpy as jnp
from jax import lax

NY = 64
NZ = 96
BLOCK = 32
LATER = 256
NX = 64


def shared_fields(key):
    return jax.random.truncated_normal(jax.random.fold_in(key, 7), -4.0, 4.0, (4, NX, NY * NZ), jnp.float32)


def envelope_field():
    xpos = lax.broadcasted_iota(jnp.float32, (NX, 1), 0) / (NX - 1)
    return 0.5 + 1.5 * xpos


def mixed_orbitals(key, count, salt):
    shared = shared_fields(key)
    noise = jax.random.truncated_normal(jax.random.fold_in(key, salt), -4.0, 4.0, (count, NX, NY * NZ), jnp.float32)
    mixing = jax.random.uniform(jax.random.fold_in(key, salt + 1), (count, 4), jnp.float32, -0.7, 0.7)
    total = noise
    for index in range(4):
        total = total + mixing[:, index, None, None] * shared[index][None]
    return total * envelope_field()[None]


def draw_blocks(key, part):
    return mixed_orbitals(key, 2 * BLOCK, 21).reshape(2, BLOCK, NX, NY * NZ)


def draw_later(key, part):
    return mixed_orbitals(key, LATER, 31)


def level_of(stream_key, shape, shards, least, largest):
    factor_of, own = 1.0, jax.random.fold_in(stream_key, 6)
    for dim, parts in shards:
        draws = jnp.exp(jax.random.uniform(jax.random.fold_in(own, dim), (parts,), jnp.float32, least / len(shards), largest / len(shards)))
        factor_of = factor_of * jnp.repeat(draws, shape[dim] // parts).reshape([-1 if axis == dim else 1 for axis in range(len(shape))])
    return factor_of


def setup_inputs(seed: int = 0) -> dict:
    keys = jax.random.split(jax.random.key(seed), 4)
    blocks = draw_blocks(jax.random.fold_in(keys[3], 71), 0)
    later = draw_later(jax.random.fold_in(keys[3], 71), 0)
    potential = jnp.clip(jax.random.uniform(keys[2], (NX, NY * NZ), jnp.float32, -1.5, 1.5) * level_of(keys[2], (NX, NY * NZ), ((0, 16),), -0.4, 0.0), -1.5, 1.5)
    return {"blocks": blocks, "later": later, "potential": potential}


stencil_weights = (-205.0 / 72.0, 8.0 / 5.0, -1.0 / 5.0, 8.0 / 315.0, -1.0 / 560.0)

def stencil(extended, potential, depth):
    center = extended[:, 4:-4]
    planes = center.shape[1]
    length = center.shape[2]
    laplace = 3.0 * stencil_weights[0] * center
    for step in range(1, 5):
        laplace = laplace + stencil_weights[step] * (extended[:, 4 + step:4 + step + planes] + extended[:, 4 - step:4 - step + planes])
    margin = 4 * depth
    ypadded = jnp.pad(center, ((0, 0), (0, 0), (margin, margin)))
    for step in range(1, 5):
        upper = ypadded[:, :, margin + step * depth:margin + step * depth + length]
        lower = ypadded[:, :, margin - step * depth:margin - step * depth + length]
        laplace = laplace + stencil_weights[step] * (upper + lower)
    zpadded = jnp.pad(center, ((0, 0), (0, 0), (4, 4)))
    zpos = lax.broadcasted_iota(jnp.int32, (length,), 0) % depth
    for step in range(1, 5):
        upper = jnp.where(zpos + step < depth, zpadded[:, :, 4 + step:4 + step + length], 0.0)
        lower = jnp.where(zpos - step >= 0, zpadded[:, :, 4 - step:4 - step + length], 0.0)
        laplace = laplace + stencil_weights[step] * (upper + lower)
    return -0.5 * laplace + potential[None] * center

def inner(left, right):
    return jnp.dot(left.astype(jnp.float32), right.T.astype(jnp.float32), precision=lax.Precision.HIGHEST, preferred_element_type=jnp.float32)

def apply_rows(left, right):
    return jnp.dot(left.astype(jnp.float32), right.astype(jnp.float32), precision=lax.Precision.HIGHEST, preferred_element_type=jnp.float32)

def reference(blocks, later, potential):
    cells = NX * NY * NZ
    flat = blocks.reshape(2, BLOCK, cells)
    first = flat[0]
    second = flat[1]
    lower_one = jnp.linalg.cholesky(inner(first, first) / cells)
    q_first = lax.linalg.triangular_solve(lower_one, first, left_side=True, lower=True)
    crossed = inner(q_first, second) / cells
    remainder = second - apply_rows(crossed.T, q_first)
    lower_two = jnp.linalg.cholesky(inner(remainder, remainder) / cells)
    q_second = lax.linalg.triangular_solve(lower_two, remainder, left_side=True, lower=True)
    basis = jnp.concatenate([q_first, q_second], axis=0)
    later_flat = later.reshape(LATER, cells)
    weights = inner(basis, later_flat) / cells
    projected = later_flat - apply_rows(weights.T, basis)
    states = jnp.concatenate([basis, projected], axis=0).reshape((2 * BLOCK + LATER) // BLOCK, BLOCK, NX, NY * NZ)

    def one_group(group):
        extended = jnp.pad(group, ((0, 0), (4, 4), (0, 0)))
        return stencil(extended, potential, NZ)
    applied = lax.map(one_group, states).reshape(2 * BLOCK + LATER, NX, NY * NZ)
    h_block = applied[:2 * BLOCK].reshape(2, BLOCK, NX, NY * NZ)
    h_later = applied[2 * BLOCK:]
    return (h_block, h_later)
```

```python
import functools

import jax
import jax.numpy as jnp
from jax import lax
from jax.experimental import pallas as pl
from jax.experimental.pallas import tpu as pltpu
from jax.sharding import PartitionSpec as P

MESH = pl.DeviceIdType.MESH
F32 = jnp.float32
BF16 = jnp.bfloat16
NZ = 96
ROWS = 192
PAD = 16
PITCH = ROWS + 2 * PAD
CHUNKS = 4
CROWS = ROWS // CHUNKS
NB = 8
NL = 32
ALL = 64
weights = (-205.0 / 72.0, 8.0 / 5.0, -1.0 / 5.0, 8.0 / 315.0, -1.0 / 560.0)


def lanes(shape=(8, 128)):
    return lax.broadcasted_iota(jnp.int32, shape, len(shape) - 1)


def split(value):
    high = value.astype(BF16)
    return high, (value - high.astype(F32)).astype(BF16)


def stencil(own, left, right, pot, group, out):
    ref, base = out
    lane = lanes()

    def load(chunk, plane):
        return own[pl.ds(group * (8 * PITCH) + PAD + 4 * chunk + plane, 8, stride=PITCH), :]

    def shifted(row, shift):
        q, e = shift // 128, shift % 128
        if e == 0:
            return row[q + 3]
        mixed = jnp.where(lane >= e, row[q + 3], row[q + 4])
        return pltpu.roll(mixed, 128 - e, 1)

    def one(chunk, third):
        zpos = lane + 32 * third
        zpos = jnp.where(zpos >= NZ, zpos - NZ, zpos)
        rows = [[load(chunk + d, plane) for d in range(-3, 4)] for plane in range(4)]
        halo = group * (8 * ROWS) + 4 * chunk
        xs = [left[pl.ds(halo + plane, 8, stride=ROWS), :] for plane in range(4)]
        xs += [rows[plane][3] for plane in range(4)]
        xs += [right[pl.ds(halo + plane, 8, stride=ROWS), :] for plane in range(4)]
        for plane in range(4):
            row = rows[plane]
            acc = (pot[pl.ds(4 * chunk + plane, 1), :] - 1.5 * weights[0]) * row[3]
            for k in range(1, 5):
                part = xs[4 + plane + k] + xs[4 + plane - k]
                part = part + (shifted(row, NZ * k) + shifted(row, -NZ * k))
                up = jnp.where(zpos < NZ - k, shifted(row, k), 0.0)
                down = jnp.where(zpos >= k, shifted(row, -k), 0.0)
                acc = acc + (-0.5 * weights[k]) * (part + (up + down))
            ref[pl.ds(base + 4 * chunk + plane, 8, stride=ROWS), :] = acc

    def body(step, carry):
        for third in range(3):
            one(3 * step + third, third)
        return carry

    lax.fori_loop(0, ROWS // 12, body, 0)


def kernel(blk, lat, pot, hb_out, hl_out,
           gath, own3, left3, right3, hown, hacc3, oblk,
           acc, gs, rbuf, red, full, m1, m2, lhs,
           loc_sem, ag_send, ag_recv, halo_send, halo_recv, rs_send, rs_recv, bc_send, bc_recv, out_sem):
    space = lax.axis_index("space")
    band = lax.axis_index("band")
    z, y = band // 4, band % 4

    def at(dy, dz):
        return lax.rem(z + dz, 2) * 4 + lax.rem(y + dy + 4, 4)

    own = own3.reshape(40 * PITCH, 128)
    left = left3.reshape(40 * ROWS, 128)
    right = right3.reshape(40 * ROWS, 128)
    hacc = hacc3.reshape(NL * ROWS, 128)
    hown2 = hown.reshape(NB * ROWS, 128)
    oblk2 = oblk.reshape(NB * ROWS, 128)
    bmat = gath.at[0].reshape(ALL * ROWS, 128)
    hmat = gath.at[1].reshape(ALL * ROWS, 128)

    barrier = pltpu.get_barrier_semaphore()
    for b in (at(1, 0), at(-1, 0), at(0, 1)):
        pl.semaphore_signal(barrier, inc=1, device_id={"band": b}, device_id_type=MESH)

    @pl.loop(1, 16)
    def _(k):
        pl.semaphore_signal(barrier, inc=1, device_id={"space": lax.rem(space + k, 16)}, device_id_type=MESH)

    local_copies = [
        pltpu.make_async_copy(blk.at[0], own3.at[pl.ds(0, 4), pl.ds(PAD, ROWS), :], loc_sem.at[0]),
        pltpu.make_async_copy(blk.at[1], own3.at[pl.ds(4, 4), pl.ds(PAD, ROWS), :], loc_sem.at[1]),
        pltpu.make_async_copy(lat, own3.at[pl.ds(8, NL), pl.ds(PAD, ROWS), :], loc_sem.at[2]),
        pltpu.make_async_copy(blk, gath.at[0, :, pl.ds(4 * band, 4), :, :], loc_sem.at[3]),
    ]
    for copy in local_copies:
        copy.start()
    pl.semaphore_wait(barrier, 18)

    def halo(part, side):
        src = blk.at[part] if part < 2 else lat.at[pl.ds(8 * (part - 2), 8)]
        first, count = (4 * part, 4) if part < 2 else (8 * (part - 1), 8)
        ref = left3 if side == 0 else right3
        return pltpu.make_async_remote_copy(
            src_ref=src, dst_ref=ref.at[pl.ds(first, count)],
            send_sem=halo_send.at[part, side], recv_sem=halo_recv.at[part, side],
            device_id={"space": space + 1 if side == 0 else space - 1}, device_id_type=MESH)

    def halo_start(parts):
        @pl.when(space < 15)
        def _():
            for part in parts:
                halo(part, 0).start()

        @pl.when(space > 0)
        def _():
            for part in parts:
                halo(part, 1).start()

    def halo_wait(parts):
        @pl.when(space > 0)
        def _():
            for part in parts:
                halo(part, 0).wait_recv()

        @pl.when(space < 15)
        def _():
            for part in parts:
                halo(part, 1).wait_recv()

    def halo_sent(parts):
        @pl.when(space < 15)
        def _():
            for part in parts:
                halo(part, 0).wait_send()

        @pl.when(space > 0)
        def _():
            for part in parts:
                halo(part, 1).wait_send()

    def slot(u, b):
        return gath.at[u // CHUNKS, :, pl.ds(4 * b, 4), pl.ds(CROWS * (u % CHUNKS), CROWS), :]

    def move(u, sid):
        even = u % 2 == 0
        source, to = {
            0: ((0, 0), (1, 0)), 1: ((0, 0), (-1, 0)), 2: ((0, 0), (0, 1)),
            3: ((-1, 0), (1, 0)) if even else ((1, 0), (-1, 0)),
            4: ((0, 1), (1, 0)), 5: ((0, 1), (-1, 0)), 6: ((2, 0), (0, 1)),
        }[sid]
        place = slot(u, at(*source))
        if sid < 3:
            part = blk if u < CHUNKS else hown
            src = part.at[:, :, pl.ds(CROWS * (u % CHUNKS), CROWS), :]
        else:
            src = place
        return pltpu.make_async_remote_copy(
            src_ref=src, dst_ref=place, send_sem=ag_send.at[u, sid], recv_sem=ag_recv.at[u, sid],
            device_id={"band": at(*to)}, device_id_type=MESH)

    def start_own(u):
        for sid in (0, 1, 2):
            move(u, sid).start()

    def forward(u):
        move(u, 2).wait_recv()
        move(u, 4).start()
        move(u, 5).start()
        move(u, 0 if u % 2 == 0 else 1).wait_recv()
        move(u, 3).start()

    def across(u):
        move(u, 3).wait_recv()
        move(u, 6).start()

    def arrived(u):
        for sid in (1 if u % 2 == 0 else 0, 4, 5, 6):
            move(u, sid).wait_recv()

    def gram(c):
        def body(step, carry):
            j4 = 4 * (12 * c + step)
            rows = jnp.concatenate([
                jnp.concatenate([bmat[pl.ds(j4 + p, ALL, stride=ROWS), :],
                                 own[pl.ds(8 * PITCH + PAD + j4 + p, NL, stride=PITCH), :]], axis=0)
                for p in range(4)], axis=1)
            high, low = split(rows)
            zero = jnp.zeros((32, 512), BF16)
            a = jnp.concatenate([high[:ALL], low[:ALL]], axis=0)
            b = jnp.concatenate([high, zero, low, zero], axis=0)
            acc[...] += lax.dot_general(a, b, (((1,), (1,)), ((), ())), preferred_element_type=F32)
            return carry

        lax.fori_loop(0, 12, body, 0)

    halo_start((0, 1))
    start_own(0)
    start_own(1)
    for copy in local_copies:
        copy.wait()

    @pl.loop(0, 40)
    def _(o):
        own3[o, pl.ds(0, PAD), :] = jnp.zeros((PAD, 128), F32)
        own3[o, pl.ds(PAD + ROWS, PAD), :] = jnp.zeros((PAD, 128), F32)

    @pl.when(space == 0)
    def _():
        left3[...] = jnp.zeros(left3.shape, F32)

    @pl.when(space == 15)
    def _():
        right3[...] = jnp.zeros(right3.shape, F32)

    acc[...] = jnp.zeros(acc.shape, F32)

    forward(0)
    start_own(2)
    halo_wait((0, 1))
    halo_start((2, 3, 4, 5))
    stencil(own, left, right, pot, 0, (hown2, 0))
    keep = pltpu.make_async_copy(hown, gath.at[1, :, pl.ds(4 * band, 4), :, :], loc_sem.at[4])
    keep.start()
    forward(1)
    across(0)
    start_own(3)
    forward(2)
    across(1)
    start_own(4)
    arrived(0)
    gram(0)
    forward(3)
    across(2)
    start_own(5)
    arrived(1)
    gram(1)
    forward(4)
    across(3)
    start_own(6)
    arrived(2)
    gram(2)
    arrived(3)
    gram(3)

    gs[...] = acc[:, :128] + acc[:, 128:]

    def scatter(k):
        peer = lax.rem(space + k, 16)
        return pltpu.make_async_remote_copy(
            src_ref=gs.at[pl.ds(8 * peer, 8), :], dst_ref=rbuf.at[space],
            send_sem=rs_send.at[k], recv_sem=rs_recv.at[k], device_id={"space": peer}, device_id_type=MESH)

    def spread(k):
        peer = lax.rem(space + k, 16)
        return pltpu.make_async_remote_copy(
            src_ref=red, dst_ref=full.at[pl.ds(8 * space, 8), :],
            send_sem=bc_send.at[k], recv_sem=bc_recv.at[k], device_id={"space": peer}, device_id_type=MESH)

    for k in range(1, 16):
        scatter(k).start()
    rbuf[pl.ds(space, 1)] = gs[pl.ds(8 * space, 8), :][None]
    forward(5)
    across(4)
    start_own(7)
    for k in range(1, 16):
        scatter(k).wait_recv()
    red[...] = jnp.sum(rbuf[...], axis=0)
    for k in range(1, 16):
        spread(k).start()
    full[pl.ds(8 * space, 8), :] = red[...]
    halo_wait((2,))
    stencil(own, left, right, pot, 1, (hacc, 0))
    for k in range(1, 16):
        spread(k).wait_recv()

    cells = 16.0 * ROWS * 128
    m1[...] = (full[pl.ds(0, ALL), :] + full[pl.ds(ALL, ALL), :]) * (1.0 / cells)
    lane64 = lanes((ALL, 128))
    row64 = lax.broadcasted_iota(jnp.int32, (ALL, 128), 0)
    m2[...] = jnp.where((lane64 == row64) | (lane64 == row64 + ALL), 1.0, 0.0).astype(F32)
    lane1 = lanes((1, 128))

    def eliminate(k, carry):
        one, two = m1[pl.ds(k, 1), :], m2[pl.ds(k, 1), :]
        pivot = jnp.sum(jnp.where(lane1 == k, one, 0.0), axis=1, keepdims=True)
        whole = m1[...]
        column = jnp.sum(jnp.where(lane64 == k, whole, 0.0), axis=1, keepdims=True)
        factor = jnp.where(row64[:, :1] > k, column / pivot, 0.0)
        m1[...] = whole - factor * one
        m2[...] = m2[...] - factor * two
        return carry

    lax.fori_loop(0, 32, eliminate, 0)
    forward(6)
    across(5)
    lax.fori_loop(32, 64, eliminate, 0)
    forward(7)
    across(6)
    diag = jnp.sum(jnp.where(lane64 == row64, m1[...], 0.0), axis=1, keepdims=True)
    scale = 1.0 / jnp.sqrt(diag)
    tri = m2[...] * scale
    proj = lax.dot_general(m1[...] * scale, tri, (((0,), (0,)), ((), ())),
                           precision=lax.Precision.HIGHEST, preferred_element_type=F32)
    row8 = lax.broadcasted_iota(jnp.int32, (8, ALL), 0)
    wanted = jnp.where(row8 < 4, row8, row8 + 28) + 4 * band
    pick = jnp.where(lanes((8, ALL)) == wanted, 1.0, 0.0).astype(F32)
    mine = jnp.dot(pick, tri, precision=lax.Precision.HIGHEST, preferred_element_type=F32)
    coef = jnp.concatenate([mine, -proj[64:96], jnp.zeros((8, 128), F32)], axis=0)
    high = coef.astype(BF16).astype(F32)
    mixed = jnp.where(lanes((48, 128)) < 64, high, coef - high).astype(BF16)
    lhs[...] = jnp.concatenate([mixed, mixed], axis=1)
    halo_wait((3, 4, 5))
    lax.fori_loop(1, 4, lambda g, carry: (
        stencil(own, left, right, pot, g + 1, (hacc, g * (8 * ROWS))), carry)[1], 0)
    across(7)
    keep.wait()

    outs = []
    for c in range(CHUNKS):
        arrived(CHUNKS + c)

        def body(step, carry, c=c):
            j4 = 4 * (12 * c + step)
            rows = jnp.concatenate([hmat[pl.ds(j4 + p, ALL, stride=ROWS), :] for p in range(4)], axis=1)
            high, low = split(rows)
            rhs = jnp.concatenate([high, high, low, low], axis=0)
            res = jnp.dot(lhs[...], rhs, preferred_element_type=F32)
            for p in range(4):
                piece = res[:, 128 * p:128 * p + 128]
                oblk2[pl.ds(j4 + p, 8, stride=ROWS), :] = piece[:8]
                for g in range(4):
                    where = pl.ds(g * (8 * ROWS) + j4 + p, 8, stride=ROWS)
                    hacc[where, :] = hacc[where, :] + piece[8 + 8 * g:16 + 8 * g]
            return carry

        lax.fori_loop(0, 12, body, 0)
        span = pl.ds(CROWS * c, CROWS)
        outs.append(pltpu.make_async_copy(oblk.at[:, :, span, :], hb_out.at[:, :, span, :], out_sem.at[0, c]))
        outs.append(pltpu.make_async_copy(hacc3.at[:, span, :], hl_out.at[:, span, :], out_sem.at[1, c]))
        outs[-2].start()
        outs[-1].start()

    halo_sent((0, 1, 2, 3, 4, 5))
    for u in range(2 * CHUNKS):
        for sid in range(7):
            move(u, sid).wait_send()
    for k in range(1, 16):
        scatter(k).wait_send()
        spread(k).wait_send()
    for copy in outs:
        copy.wait()


def rows_of(x):
    lead = x.shape[:-2]
    x = x.reshape(*lead, 4, 48, 128)
    return jnp.swapaxes(x, -3, -2).reshape(*lead, ROWS, 128)


def planes_of(x):
    lead = x.shape[:-2]
    x = jnp.swapaxes(x.reshape(*lead, 48, 4, 128), -3, -2)
    return x.reshape(*lead, 4, 48 * 128)


def local(blocks, later, potential):
    hb, hl = pl.pallas_call(
        kernel,
        out_shape=[jax.ShapeDtypeStruct((2, 4, ROWS, 128), F32), jax.ShapeDtypeStruct((NL, ROWS, 128), F32)],
        in_specs=[pl.BlockSpec(memory_space=pl.ANY), pl.BlockSpec(memory_space=pl.ANY),
                  pl.BlockSpec(memory_space=pltpu.VMEM)],
        out_specs=[pl.BlockSpec(memory_space=pl.ANY), pl.BlockSpec(memory_space=pl.ANY)],
        scratch_shapes=[
            pltpu.VMEM((2, 2, 32, ROWS, 128), F32),
            pltpu.VMEM((40, PITCH, 128), F32),
            pltpu.VMEM((40, ROWS, 128), F32),
            pltpu.VMEM((40, ROWS, 128), F32),
            pltpu.VMEM((2, 4, ROWS, 128), F32),
            pltpu.VMEM((NL, ROWS, 128), F32),
            pltpu.VMEM((2, 4, ROWS, 128), F32),
            pltpu.VMEM((128, 256), F32),
            pltpu.VMEM((128, 128), F32),
            pltpu.VMEM((16, 8, 128), F32),
            pltpu.VMEM((8, 128), F32),
            pltpu.VMEM((128, 128), F32),
            pltpu.VMEM((ALL, 128), F32),
            pltpu.VMEM((ALL, 128), F32),
            pltpu.VMEM((48, 256), BF16),
            pltpu.SemaphoreType.DMA((5,)),
            pltpu.SemaphoreType.DMA((8, 7)),
            pltpu.SemaphoreType.DMA((8, 7)),
            pltpu.SemaphoreType.DMA((6, 2)),
            pltpu.SemaphoreType.DMA((6, 2)),
            pltpu.SemaphoreType.DMA((16,)),
            pltpu.SemaphoreType.DMA((16,)),
            pltpu.SemaphoreType.DMA((16,)),
            pltpu.SemaphoreType.DMA((16,)),
            pltpu.SemaphoreType.DMA((2, 4)),
        ],
        compiler_params=pltpu.CompilerParams(
            collective_id=0, has_side_effects=True, vmem_limit_bytes=56 * 1024 * 1024),
    )(rows_of(blocks), rows_of(later), rows_of(potential))
    return planes_of(hb), planes_of(hl)


def solution(mesh):
    return jax.shard_map(
        local,
        mesh=mesh,
        in_specs=(P(None, "band", "space", None), P("band", "space", None), P("space", None)),
        out_specs=(P(None, "band", "space", None), P("band", "space", None)),
        check_vma=False,
    )
```

```python
import functools

import jax
import jax.numpy as jnp
from jax import lax
from jax.experimental import pallas as pl
from jax.experimental.pallas import tpu as pltpu
from jax.sharding import PartitionSpec as P

MESH = pl.DeviceIdType.MESH
F32 = jnp.float32
BF16 = jnp.bfloat16
NZ = 96
ROWS = 192
PAD = 16
PITCH = ROWS + 2 * PAD
CHUNKS = 4
CROWS = ROWS // CHUNKS
NB = 8
NL = 32
VIA = 5
ALL = 64
weights = (-205.0 / 72.0, 8.0 / 5.0, -1.0 / 5.0, 8.0 / 315.0, -1.0 / 560.0)


def lanes(shape=(8, 128)):
    return lax.broadcasted_iota(jnp.int32, shape, len(shape) - 1)


def split(value):
    high = value.astype(BF16)
    return high, (value - high.astype(F32)).astype(BF16)


def stencil(own, left, right, pot, group, out):
    ref, base = out
    lane = lanes()

    def load(chunk, plane):
        return own[pl.ds(group * (8 * PITCH) + PAD + 4 * chunk + plane, 8, stride=PITCH), :]

    def shifted(row, shift):
        q, e = shift // 128, shift % 128
        if e == 0:
            return row[q + 3]
        mixed = jnp.where(lane >= e, row[q + 3], row[q + 4])
        return pltpu.roll(mixed, 128 - e, 1)

    def one(chunk, third):
        zpos = lane + 32 * third
        zpos = jnp.where(zpos >= NZ, zpos - NZ, zpos)
        rows = [[load(chunk + d, plane) for d in range(-3, 4)] for plane in range(4)]
        halo = group * (8 * ROWS) + 4 * chunk
        xs = [left[pl.ds(halo + plane, 8, stride=ROWS), :] for plane in range(4)]
        xs += [rows[plane][3] for plane in range(4)]
        xs += [right[pl.ds(halo + plane, 8, stride=ROWS), :] for plane in range(4)]
        for plane in range(4):
            row = rows[plane]
            acc = (pot[pl.ds(4 * chunk + plane, 1), :] - 1.5 * weights[0]) * row[3]
            for k in range(1, 5):
                part = xs[4 + plane + k] + xs[4 + plane - k]
                part = part + (shifted(row, NZ * k) + shifted(row, -NZ * k))
                up = jnp.where(zpos < NZ - k, shifted(row, k), 0.0)
                down = jnp.where(zpos >= k, shifted(row, -k), 0.0)
                acc = acc + (-0.5 * weights[k]) * (part + (up + down))
            ref[pl.ds(base + 4 * chunk + plane, 8, stride=ROWS), :] = acc

    def body(step, carry):
        for third in range(3):
            one(3 * step + third, third)
        return carry

    lax.fori_loop(0, ROWS // 12, body, 0)


def kernel(blk, lat, pot, hb_out, hl_out,
           gath, own3, left3, right3, relay, hown, hacc3, oblk,
           acc, gs, rbuf, red, full, m1, m2, lhs,
           loc_sem, ag_send, ag_recv, halo_send, halo_recv, relay_send, relay_recv, rs_send, rs_recv, bc_send, bc_recv, out_sem):
    space = lax.axis_index("space")
    band = lax.axis_index("band")
    z, y = band // 4, band % 4

    def at(dy, dz):
        return lax.rem(z + dz, 2) * 4 + lax.rem(y + dy + 4, 4)

    own = own3.reshape(40 * PITCH, 128)
    left = left3.reshape(40 * ROWS, 128)
    right = right3.reshape(40 * ROWS, 128)
    hacc = hacc3.reshape(NL * ROWS, 128)
    hown2 = hown.reshape(NB * ROWS, 128)
    oblk2 = oblk.reshape(NB * ROWS, 128)
    bmat = gath.at[0].reshape(ALL * ROWS, 128)
    hmat = gath.at[1].reshape(ALL * ROWS, 128)

    barrier = pltpu.get_barrier_semaphore()
    for b in (at(1, 0), at(-1, 0), at(0, 1)):
        pl.semaphore_signal(barrier, inc=1, device_id={"band": b}, device_id_type=MESH)

    @pl.loop(1, 16)
    def _(k):
        pl.semaphore_signal(barrier, inc=1, device_id={"space": lax.rem(space + k, 16)}, device_id_type=MESH)

    local_copies = [
        pltpu.make_async_copy(blk.at[0], own3.at[pl.ds(0, 4), pl.ds(PAD, ROWS), :], loc_sem.at[0]),
        pltpu.make_async_copy(blk.at[1], own3.at[pl.ds(4, 4), pl.ds(PAD, ROWS), :], loc_sem.at[1]),
        pltpu.make_async_copy(lat, own3.at[pl.ds(8, NL), pl.ds(PAD, ROWS), :], loc_sem.at[2]),
        pltpu.make_async_copy(blk, gath.at[0, :, pl.ds(4 * band, 4), :, :], loc_sem.at[3]),
    ]
    for copy in local_copies:
        copy.start()
    pl.semaphore_wait(barrier, 18)

    def source(part):
        return blk.at[part] if part < 2 else lat.at[pl.ds(4 * (part - 2), 4)]

    def halo(part, side):
        ref = left3 if side == 0 else right3
        return pltpu.make_async_remote_copy(
            src_ref=source(part), dst_ref=ref.at[pl.ds(4 * part, 4)],
            send_sem=halo_send.at[part, side], recv_sem=halo_recv.at[part, side],
            device_id={"space": space + 1 if side == 0 else space - 1}, device_id_type=MESH)

    def detour(part, side):
        return pltpu.make_async_remote_copy(
            src_ref=source(part), dst_ref=relay.at[part - VIA],
            send_sem=halo_send.at[part, side], recv_sem=relay_recv.at[part - VIA],
            device_id={"space": space + 8 if side == 0 else space - 8}, device_id_type=MESH)

    def onward(part, side):
        ref = left3 if side == 0 else right3
        return pltpu.make_async_remote_copy(
            src_ref=relay.at[part - VIA], dst_ref=ref.at[pl.ds(4 * part, 4)],
            send_sem=relay_send.at[part - VIA], recv_sem=halo_recv.at[part, side],
            device_id={"space": space - 7 if side == 0 else space + 7}, device_id_type=MESH)

    senders = ((space < 15, space == 7, space != 7), (space > 0, space == 8, space != 8))

    def halo_each(parts, direct, around):
        for side, (any_, seam, inner) in enumerate(senders):
            @pl.when(any_)
            def _(side=side):
                for part in parts:
                    if part < VIA:
                        direct(part, side)

            if any(part >= VIA for part in parts):
                @pl.when(any_ & inner)
                def _(side=side):
                    for part in parts:
                        if part >= VIA:
                            direct(part, side)

                @pl.when(seam)
                def _(side=side):
                    for part in parts:
                        if part >= VIA:
                            around(part, side)

    def halo_start(parts):
        halo_each(parts, lambda p, s: halo(p, s).start(), lambda p, s: detour(p, s).start())

    def halo_sent(parts):
        halo_each(parts, lambda p, s: halo(p, s).wait_send(), lambda p, s: detour(p, s).wait_send())

    def halo_wait(parts):
        for side, there in enumerate((space > 0, space < 15)):
            @pl.when(there)
            def _(side=side):
                for part in parts:
                    halo(part, side).wait_recv()

    def pass_on(parts):
        for side, here in enumerate((space == 15, space == 0)):
            @pl.when(here)
            def _(side=side):
                for part in parts:
                    detour(part, side).wait_recv()
                    onward(part, side).start()

    def passed(parts):
        for side, here in enumerate((space == 15, space == 0)):
            @pl.when(here)
            def _(side=side):
                for part in parts:
                    onward(part, side).wait_send()

    def slot(u, b):
        return gath.at[u // CHUNKS, :, pl.ds(4 * b, 4), pl.ds(CROWS * (u % CHUNKS), CROWS), :]

    def move(u, sid):
        even = u % 2 == 0
        source, to = {
            0: ((0, 0), (1, 0)), 1: ((0, 0), (-1, 0)), 2: ((0, 0), (0, 1)),
            3: ((-1, 0), (1, 0)) if even else ((1, 0), (-1, 0)),
            4: ((0, 1), (1, 0)), 5: ((0, 1), (-1, 0)), 6: ((2, 0), (0, 1)),
        }[sid]
        place = slot(u, at(*source))
        if sid < 3:
            part = blk if u < CHUNKS else hown
            src = part.at[:, :, pl.ds(CROWS * (u % CHUNKS), CROWS), :]
        else:
            src = place
        return pltpu.make_async_remote_copy(
            src_ref=src, dst_ref=place, send_sem=ag_send.at[u, sid], recv_sem=ag_recv.at[u, sid],
            device_id={"band": at(*to)}, device_id_type=MESH)

    def start_own(u):
        for sid in (0, 1, 2):
            move(u, sid).start()

    def forward(u):
        move(u, 2).wait_recv()
        move(u, 4).start()
        move(u, 5).start()
        move(u, 0 if u % 2 == 0 else 1).wait_recv()
        move(u, 3).start()

    def across(u):
        move(u, 3).wait_recv()
        move(u, 6).start()

    def arrived(u):
        for sid in (1 if u % 2 == 0 else 0, 4, 5, 6):
            move(u, sid).wait_recv()

    def gram(c):
        def body(step, carry):
            j4 = 4 * (12 * c + step)
            rows = jnp.concatenate([
                jnp.concatenate([bmat[pl.ds(j4 + p, ALL, stride=ROWS), :],
                                 own[pl.ds(8 * PITCH + PAD + j4 + p, NL, stride=PITCH), :]], axis=0)
                for p in range(4)], axis=1)
            high, low = split(rows)
            zero = jnp.zeros((32, 512), BF16)
            a = jnp.concatenate([high[:ALL], low[:ALL]], axis=0)
            b = jnp.concatenate([high, zero, low, zero], axis=0)
            acc[...] += lax.dot_general(a, b, (((1,), (1,)), ((), ())), preferred_element_type=F32)
            return carry

        lax.fori_loop(0, 12, body, 0)

    start_own(0)
    halo_start(range(10))
    start_own(1)
    for copy in local_copies:
        copy.wait()

    @pl.loop(0, 40)
    def _(o):
        own3[o, pl.ds(0, PAD), :] = jnp.zeros((PAD, 128), F32)
        own3[o, pl.ds(PAD + ROWS, PAD), :] = jnp.zeros((PAD, 128), F32)

    @pl.when(space == 0)
    def _():
        left3[...] = jnp.zeros(left3.shape, F32)

    @pl.when(space == 15)
    def _():
        right3[...] = jnp.zeros(right3.shape, F32)

    acc[...] = jnp.zeros(acc.shape, F32)

    def later(g):
        halo_wait((2 * g, 2 * g + 1))
        stencil(own, left, right, pot, g, (hacc, (g - 1) * (8 * ROWS)))

    forward(0)
    start_own(2)
    forward(1)
    across(0)
    start_own(3)
    halo_wait((0, 1))
    stencil(own, left, right, pot, 0, (hown2, 0))
    keep = pltpu.make_async_copy(hown, gath.at[1, :, pl.ds(4 * band, 4), :, :], loc_sem.at[4])
    keep.start()
    forward(2)
    across(1)
    start_own(4)
    arrived(0)
    gram(0)
    forward(3)
    across(2)
    start_own(5)
    arrived(1)
    gram(1)
    forward(4)
    across(3)
    start_own(6)
    pass_on((5,))
    arrived(2)
    gram(2)
    arrived(3)
    gram(3)

    gs[...] = acc[:, :128] + acc[:, 128:]

    def scatter(k):
        peer = lax.rem(space + k, 16)
        return pltpu.make_async_remote_copy(
            src_ref=gs.at[pl.ds(8 * peer, 8), :], dst_ref=rbuf.at[space],
            send_sem=rs_send.at[k], recv_sem=rs_recv.at[k], device_id={"space": peer}, device_id_type=MESH)

    def spread(k):
        peer = lax.rem(space + k, 16)
        return pltpu.make_async_remote_copy(
            src_ref=red, dst_ref=full.at[pl.ds(8 * space, 8), :],
            send_sem=bc_send.at[k], recv_sem=bc_recv.at[k], device_id={"space": peer}, device_id_type=MESH)

    for k in range(1, 16):
        scatter(k).start()
    rbuf[pl.ds(space, 1)] = gs[pl.ds(8 * space, 8), :][None]
    later(1)
    for k in range(1, 16):
        scatter(k).wait_recv()
    red[...] = jnp.sum(rbuf[...], axis=0)
    for k in range(1, 16):
        spread(k).start()
    full[pl.ds(8 * space, 8), :] = red[...]
    forward(5)
    across(4)
    start_own(7)
    pass_on((6, 7))
    later(2)
    for k in range(1, 16):
        spread(k).wait_recv()

    cells = 16.0 * ROWS * 128
    m1[...] = (full[pl.ds(0, ALL), :] + full[pl.ds(ALL, ALL), :]) * (1.0 / cells)
    lane64 = lanes((ALL, 128))
    row64 = lax.broadcasted_iota(jnp.int32, (ALL, 128), 0)
    m2[...] = jnp.where((lane64 == row64) | (lane64 == row64 + ALL), 1.0, 0.0).astype(F32)
    lane1 = lanes((1, 128))

    def eliminate(k, carry):
        one, two = m1[pl.ds(k, 1), :], m2[pl.ds(k, 1), :]
        pivot = jnp.sum(jnp.where(lane1 == k, one, 0.0), axis=1, keepdims=True)
        whole = m1[...]
        column = jnp.sum(jnp.where(lane64 == k, whole, 0.0), axis=1, keepdims=True)
        factor = jnp.where(row64[:, :1] > k, column / pivot, 0.0)
        m1[...] = whole - factor * one
        m2[...] = m2[...] - factor * two
        return carry

    lax.fori_loop(0, 32, eliminate, 0)
    forward(6)
    across(5)
    pass_on((8, 9))
    lax.fori_loop(32, 64, eliminate, 0)
    diag = jnp.sum(jnp.where(lane64 == row64, m1[...], 0.0), axis=1, keepdims=True)
    scale = 1.0 / jnp.sqrt(diag)
    tri = m2[...] * scale
    proj = lax.dot_general(m1[...] * scale, tri, (((0,), (0,)), ((), ())),
                           precision=lax.Precision.HIGHEST, preferred_element_type=F32)
    row8 = lax.broadcasted_iota(jnp.int32, (8, ALL), 0)
    wanted = jnp.where(row8 < 4, row8, row8 + 28) + 4 * band
    pick = jnp.where(lanes((8, ALL)) == wanted, 1.0, 0.0).astype(F32)
    mine = jnp.dot(pick, tri, precision=lax.Precision.HIGHEST, preferred_element_type=F32)
    coef = jnp.concatenate([mine, -proj[64:96], jnp.zeros((8, 128), F32)], axis=0)
    high = coef.astype(BF16).astype(F32)
    mixed = jnp.where(lanes((48, 128)) < 64, high, coef - high).astype(BF16)
    lhs[...] = jnp.concatenate([mixed, mixed], axis=1)
    later(3)
    forward(7)
    across(6)
    later(4)
    across(7)
    keep.wait()

    outs = []
    for c in range(CHUNKS):
        arrived(CHUNKS + c)

        def body(step, carry, c=c):
            j4 = 4 * (12 * c + step)
            rows = jnp.concatenate([hmat[pl.ds(j4 + p, ALL, stride=ROWS), :] for p in range(4)], axis=1)
            high, low = split(rows)
            rhs = jnp.concatenate([high, high, low, low], axis=0)
            res = jnp.dot(lhs[...], rhs, preferred_element_type=F32)
            for p in range(4):
                piece = res[:, 128 * p:128 * p + 128]
                oblk2[pl.ds(j4 + p, 8, stride=ROWS), :] = piece[:8]
                for g in range(4):
                    where = pl.ds(g * (8 * ROWS) + j4 + p, 8, stride=ROWS)
                    hacc[where, :] = hacc[where, :] + piece[8 + 8 * g:16 + 8 * g]
            return carry

        lax.fori_loop(0, 12, body, 0)
        span = pl.ds(CROWS * c, CROWS)
        outs.append(pltpu.make_async_copy(oblk.at[:, :, span, :], hb_out.at[:, :, span, :], out_sem.at[0, c]))
        outs.append(pltpu.make_async_copy(hacc3.at[:, span, :], hl_out.at[:, span, :], out_sem.at[1, c]))
        outs[-2].start()
        outs[-1].start()

    halo_sent(range(10))
    passed(range(VIA, 10))
    for u in range(2 * CHUNKS):
        for sid in range(7):
            move(u, sid).wait_send()
    for k in range(1, 16):
        scatter(k).wait_send()
        spread(k).wait_send()
    for copy in outs:
        copy.wait()


def rows_of(x):
    lead = x.shape[:-2]
    x = x.reshape(*lead, 4, 48, 128)
    return jnp.swapaxes(x, -3, -2).reshape(*lead, ROWS, 128)


def planes_of(x):
    lead = x.shape[:-2]
    x = jnp.swapaxes(x.reshape(*lead, 48, 4, 128), -3, -2)
    return x.reshape(*lead, 4, 48 * 128)


def local(blocks, later, potential):
    hb, hl = pl.pallas_call(
        kernel,
        out_shape=[jax.ShapeDtypeStruct((2, 4, ROWS, 128), F32), jax.ShapeDtypeStruct((NL, ROWS, 128), F32)],
        in_specs=[pl.BlockSpec(memory_space=pl.ANY), pl.BlockSpec(memory_space=pl.ANY),
                  pl.BlockSpec(memory_space=pltpu.VMEM)],
        out_specs=[pl.BlockSpec(memory_space=pl.ANY), pl.BlockSpec(memory_space=pl.ANY)],
        scratch_shapes=[
            pltpu.VMEM((2, 2, 32, ROWS, 128), F32),
            pltpu.VMEM((40, PITCH, 128), F32),
            pltpu.VMEM((40, ROWS, 128), F32),
            pltpu.VMEM((40, ROWS, 128), F32),
            pltpu.VMEM((10 - VIA, 4, ROWS, 128), F32),
            pltpu.VMEM((2, 4, ROWS, 128), F32),
            pltpu.VMEM((NL, ROWS, 128), F32),
            pltpu.VMEM((2, 4, ROWS, 128), F32),
            pltpu.VMEM((128, 256), F32),
            pltpu.VMEM((128, 128), F32),
            pltpu.VMEM((16, 8, 128), F32),
            pltpu.VMEM((8, 128), F32),
            pltpu.VMEM((128, 128), F32),
            pltpu.VMEM((ALL, 128), F32),
            pltpu.VMEM((ALL, 128), F32),
            pltpu.VMEM((48, 256), BF16),
            pltpu.SemaphoreType.DMA((5,)),
            pltpu.SemaphoreType.DMA((8, 7)),
            pltpu.SemaphoreType.DMA((8, 7)),
            pltpu.SemaphoreType.DMA((10, 2)),
            pltpu.SemaphoreType.DMA((10, 2)),
            pltpu.SemaphoreType.DMA((10 - VIA,)),
            pltpu.SemaphoreType.DMA((10 - VIA,)),
            pltpu.SemaphoreType.DMA((16,)),
            pltpu.SemaphoreType.DMA((16,)),
            pltpu.SemaphoreType.DMA((16,)),
            pltpu.SemaphoreType.DMA((16,)),
            pltpu.SemaphoreType.DMA((2, 4)),
        ],
        compiler_params=pltpu.CompilerParams(
            collective_id=0, has_side_effects=True, vmem_limit_bytes=56 * 1024 * 1024),
    )(rows_of(blocks), rows_of(later), rows_of(potential))
    return planes_of(hb), planes_of(hl)


def solution(mesh):
    return jax.shard_map(
        local,
        mesh=mesh,
        in_specs=(P(None, "band", "space", None), P("band", "space", None), P("space", None)),
        out_specs=(P(None, "band", "space", None), P("band", "space", None)),
        check_vma=False,
    )
```

```python
import functools

import jax
import jax.numpy as jnp
from jax import lax
from jax.experimental import pallas as pl
from jax.experimental.pallas import tpu as pltpu
from jax.sharding import PartitionSpec as P

MESH = pl.DeviceIdType.MESH
F32 = jnp.float32
BF16 = jnp.bfloat16
NZ = 96
ROWS = 192
PAD = 16
PITCH = 216
STEP = 200
CHUNKS = 6
CROWS = ROWS // CHUNKS
UNITS = 2 * CHUNKS
HALOS = {0: (0, 1, 5), 1: (6, 2), 2: (7, 3), 3: (8, 4), 4: (9,)}
PASSES = {6: (5,), 7: (6,), 8: (7,), 9: (8,), 10: (9,)}
NB = 8
NL = 32
VIA = 5
ALL = 64
weights = (-205.0 / 72.0, 8.0 / 5.0, -1.0 / 5.0, 8.0 / 315.0, -1.0 / 560.0)


def lanes(shape=(8, 128)):
    return lax.broadcasted_iota(jnp.int32, shape, len(shape) - 1)


def split(value):
    high = value.astype(BF16)
    return high, (value - high.astype(F32)).astype(BF16)


def stencil(own, left, right, pot, group, out):
    ref, base = out
    lane = lanes()

    def load(chunk, plane):
        return own[pl.ds(group * (8 * PITCH) + PAD + 4 * chunk + plane, 8, stride=PITCH), :]

    def shifted(row, shift):
        q, e = shift // 128, shift % 128
        if e == 0:
            return row[q + 3]
        mixed = jnp.where(lane >= e, row[q + 3], row[q + 4])
        return pltpu.roll(mixed, 128 - e, 1)

    def one(chunk, third):
        zpos = lane + 32 * third
        zpos = jnp.where(zpos >= NZ, zpos - NZ, zpos)
        rows = [[load(chunk + d, plane) for d in range(-3, 4)] for plane in range(4)]
        halo = group * (8 * STEP) + 4 * chunk
        xs = [left[pl.ds(halo + plane, 8, stride=STEP), :] for plane in range(4)]
        xs += [rows[plane][3] for plane in range(4)]
        xs += [right[pl.ds(halo + plane, 8, stride=STEP), :] for plane in range(4)]
        for plane in range(4):
            row = rows[plane]
            acc = (pot[pl.ds(4 * chunk + plane, 1), :] - 1.5 * weights[0]) * row[3]
            for k in range(1, 5):
                part = xs[4 + plane + k] + xs[4 + plane - k]
                part = part + (shifted(row, NZ * k) + shifted(row, -NZ * k))
                up = jnp.where(zpos < NZ - k, shifted(row, k), 0.0)
                down = jnp.where(zpos >= k, shifted(row, -k), 0.0)
                acc = acc + (-0.5 * weights[k]) * (part + (up + down))
            ref[pl.ds(base + 4 * chunk + plane, 8, stride=STEP), :] = acc

    def body(step, carry):
        for third in range(3):
            one(3 * step + third, third)
        return carry

    lax.fori_loop(0, ROWS // 12, body, 0)


def kernel(blk, lat, pot, hb_out, hl_out,
           gath, own3, left3, right3, relay, hown, hacc3, oblk,
           acc, gs, rbuf, red, full, m1, m2, lhs,
           loc_sem, ag_send, ag_recv, halo_send, halo_recv, relay_send, relay_recv, rs_send, rs_recv, bc_send, bc_recv, out_sem):
    space = lax.axis_index("space")
    band = lax.axis_index("band")
    z, y = band // 4, band % 4

    def at(dy, dz):
        return lax.rem(z + dz, 2) * 4 + lax.rem(y + dy + 4, 4)

    own = own3.reshape(41 * PITCH, 128)
    left = left3.reshape(40 * STEP, 128)
    right = right3.reshape(40 * STEP, 128)
    hacc = hacc3.reshape(NL * STEP, 128)
    hown2 = hown.reshape(NB * STEP, 128)
    oblk2 = oblk.reshape(NB * STEP, 128)
    bmat = gath.at[0].reshape(ALL * STEP, 128)
    hmat = gath.at[1].reshape(ALL * STEP, 128)

    barrier = pltpu.get_barrier_semaphore()
    for b in (at(1, 0), at(-1, 0), at(0, 1)):
        pl.semaphore_signal(barrier, inc=1, device_id={"band": b}, device_id_type=MESH)

    @pl.loop(1, 16)
    def _(k):
        pl.semaphore_signal(barrier, inc=1, device_id={"space": lax.rem(space + k, 16)}, device_id_type=MESH)

    local_copies = [
        pltpu.make_async_copy(blk.at[0], own3.at[pl.ds(0, 4), pl.ds(PAD, ROWS), :], loc_sem.at[0]),
        pltpu.make_async_copy(blk.at[1], own3.at[pl.ds(4, 4), pl.ds(PAD, ROWS), :], loc_sem.at[1]),
        pltpu.make_async_copy(lat, own3.at[pl.ds(8, NL), pl.ds(PAD, ROWS), :], loc_sem.at[2]),
        pltpu.make_async_copy(blk, gath.at[0, :, pl.ds(4 * band, 4), pl.ds(0, ROWS), :], loc_sem.at[3]),
    ]
    for copy in local_copies:
        copy.start()
    pl.semaphore_wait(barrier, 18)

    def source(part):
        return blk.at[part] if part < 2 else lat.at[pl.ds(4 * (part - 2), 4)]

    def halo(part, side):
        ref = left3 if side == 0 else right3
        return pltpu.make_async_remote_copy(
            src_ref=source(part), dst_ref=ref.at[pl.ds(4 * part, 4), pl.ds(0, ROWS), :],
            send_sem=halo_send.at[part, side], recv_sem=halo_recv.at[part, side],
            device_id={"space": space + 1 if side == 0 else space - 1}, device_id_type=MESH)

    def detour(part, side):
        return pltpu.make_async_remote_copy(
            src_ref=source(part), dst_ref=relay.at[part - VIA],
            send_sem=halo_send.at[part, side], recv_sem=relay_recv.at[part - VIA],
            device_id={"space": space + 8 if side == 0 else space - 8}, device_id_type=MESH)

    def onward(part, side):
        ref = left3 if side == 0 else right3
        return pltpu.make_async_remote_copy(
            src_ref=relay.at[part - VIA], dst_ref=ref.at[pl.ds(4 * part, 4), pl.ds(0, ROWS), :],
            send_sem=relay_send.at[part - VIA], recv_sem=halo_recv.at[part, side],
            device_id={"space": space - 7 if side == 0 else space + 7}, device_id_type=MESH)

    senders = ((space < 15, space == 7, space != 7), (space > 0, space == 8, space != 8))

    def halo_each(parts, direct, around):
        for side, (any_, seam, inner) in enumerate(senders):
            @pl.when(any_)
            def _(side=side):
                for part in parts:
                    if part < VIA:
                        direct(part, side)

            if any(part >= VIA for part in parts):
                @pl.when(any_ & inner)
                def _(side=side):
                    for part in parts:
                        if part >= VIA:
                            direct(part, side)

                @pl.when(seam)
                def _(side=side):
                    for part in parts:
                        if part >= VIA:
                            around(part, side)

    def halo_start(parts):
        halo_each(parts, lambda p, s: halo(p, s).start(), lambda p, s: detour(p, s).start())

    def halo_sent(parts):
        halo_each(parts, lambda p, s: halo(p, s).wait_send(), lambda p, s: detour(p, s).wait_send())

    def halo_wait(parts):
        for side, there in enumerate((space > 0, space < 15)):
            @pl.when(there)
            def _(side=side):
                for part in parts:
                    halo(part, side).wait_recv()

    def pass_on(parts):
        for side, here in enumerate((space == 15, space == 0)):
            @pl.when(here)
            def _(side=side):
                for part in parts:
                    detour(part, side).wait_recv()
                    onward(part, side).start()

    def passed(parts):
        for side, here in enumerate((space == 15, space == 0)):
            @pl.when(here)
            def _(side=side):
                for part in parts:
                    onward(part, side).wait_send()

    def slot(u, b):
        return gath.at[u // CHUNKS, :, pl.ds(4 * b, 4), pl.ds(CROWS * (u % CHUNKS), CROWS), :]

    def move(u, sid):
        even = u % 2 == 0
        source, to = {
            0: ((0, 0), (1, 0)), 1: ((0, 0), (-1, 0)), 2: ((0, 0), (0, 1)),
            3: ((-1, 0), (1, 0)) if even else ((1, 0), (-1, 0)),
            4: ((0, 1), (1, 0)), 5: ((0, 1), (-1, 0)), 6: ((2, 0), (0, 1)),
        }[sid]
        place = slot(u, at(*source))
        if sid < 3:
            part = blk if u < CHUNKS else hown
            src = part.at[:, :, pl.ds(CROWS * (u % CHUNKS), CROWS), :]
        else:
            src = place
        return pltpu.make_async_remote_copy(
            src_ref=src, dst_ref=place, send_sem=ag_send.at[u, sid], recv_sem=ag_recv.at[u, sid],
            device_id={"band": at(*to)}, device_id_type=MESH)

    def start_own(u):
        for sid in (0, 1, 2):
            move(u, sid).start()

    def forward(u):
        move(u, 2).wait_recv()
        move(u, 4).start()
        move(u, 5).start()
        move(u, 0 if u % 2 == 0 else 1).wait_recv()
        move(u, 3).start()

    def across(u):
        move(u, 3).wait_recv()
        move(u, 6).start()

    def arrived(u):
        for sid in (1 if u % 2 == 0 else 0, 4, 5, 6):
            move(u, sid).wait_recv()

    def gram(c):
        def body(step, carry):
            j4 = CROWS * c + 4 * step
            rows = jnp.concatenate([
                jnp.concatenate([bmat[pl.ds(j4 + p, ALL, stride=STEP), :],
                                 own[pl.ds(8 * PITCH + PAD + j4 + p, NL, stride=PITCH), :]], axis=0)
                for p in range(4)], axis=1)
            high, low = split(rows)
            a = jnp.concatenate([high, low], axis=0)
            b = jnp.concatenate([high[:ALL], low[:ALL]], axis=0)
            acc[...] += lax.dot_general(a, b, (((1,), (1,)), ((), ())), preferred_element_type=F32)
            return carry

        lax.fori_loop(0, CROWS // 4, body, 0)

    start_own(0)
    start_own(1)
    for copy in local_copies:
        copy.wait()

    @pl.loop(0, 41)
    def _(o):
        own3[o, pl.ds(0, PAD), :] = jnp.zeros((PAD, 128), F32)
        own3[o, pl.ds(PAD + ROWS, 8), :] = jnp.zeros((8, 128), F32)

    @pl.when(space == 0)
    def _():
        left3[...] = jnp.zeros(left3.shape, F32)

    @pl.when(space == 15)
    def _():
        right3[...] = jnp.zeros(right3.shape, F32)

    acc[...] = jnp.zeros(acc.shape, F32)

    def later(g):
        halo_wait((2 * g, 2 * g + 1))
        stencil(own, left, right, pot, g, (hacc, (g - 1) * (8 * STEP)))

    def step(t):
        if t < UNITS:
            forward(t)
        if 1 <= t:
            across(t - 1)
        if t + 2 < UNITS:
            start_own(t + 2)
        halo_start(HALOS.get(t, ()))
        pass_on(PASSES.get(t, ()))

    for t in range(CHUNKS - 2):
        step(t)
        if t >= 2:
            arrived(t - 2)
            gram(t - 2)
        if t == CHUNKS - 3:
            halo_wait((0, 1))
            stencil(own, left, right, pot, 0, (hown2, 0))
            keep = pltpu.make_async_copy(hown.at[:, :, pl.ds(0, ROWS), :], gath.at[1, :, pl.ds(4 * band, 4), pl.ds(0, ROWS), :],
                                         loc_sem.at[4])
            keep.start()
    for t in range(CHUNKS - 2, CHUNKS + 2):
        step(t)
        if t == CHUNKS:
            later(1)
        arrived(t - 2)
        gram(t - 2)

    gs[pl.ds(0, 96), :] = acc[:96] + acc[96:]
    gs[pl.ds(96, 32), :] = jnp.zeros((32, 128), F32)

    def scatter(k):
        peer = lax.rem(space + k, 16)
        return pltpu.make_async_remote_copy(
            src_ref=gs.at[pl.ds(8 * peer, 8), :], dst_ref=rbuf.at[space],
            send_sem=rs_send.at[k], recv_sem=rs_recv.at[k], device_id={"space": peer}, device_id_type=MESH)

    def spread(k):
        peer = lax.rem(space + k, 16)
        return pltpu.make_async_remote_copy(
            src_ref=red, dst_ref=full.at[pl.ds(8 * space, 8), :],
            send_sem=bc_send.at[k], recv_sem=bc_recv.at[k], device_id={"space": peer}, device_id_type=MESH)

    for k in range(1, 16):
        scatter(k).start()
    rbuf[pl.ds(space, 1)] = gs[pl.ds(8 * space, 8), :][None]
    later(2)
    step(CHUNKS + 2)
    for k in range(1, 16):
        scatter(k).wait_recv()
    red[...] = jnp.sum(rbuf[...], axis=0)
    for k in range(1, 16):
        spread(k).start()
    full[pl.ds(8 * space, 8), :] = red[...]
    later(3)
    step(CHUNKS + 3)
    for k in range(1, 16):
        spread(k).wait_recv()

    cells = 16.0 * ROWS * 128
    total = full[...]
    m1[...] = jnp.transpose(total + pltpu.roll(total, ALL, 1))[:ALL] * (1.0 / cells)
    lane64 = lanes((ALL, 128))
    row64 = lax.broadcasted_iota(jnp.int32, (ALL, 128), 0)
    m2[...] = jnp.where((lane64 == row64) | (lane64 == row64 + ALL), 1.0, 0.0).astype(F32)
    lane1 = lanes((1, 128))

    def eliminate(k, carry):
        one, two = m1[pl.ds(k, 1), :], m2[pl.ds(k, 1), :]
        pivot = jnp.sum(jnp.where(lane1 == k, one, 0.0), axis=1, keepdims=True)
        whole = m1[...]
        column = jnp.sum(jnp.where(lane64 == k, whole, 0.0), axis=1, keepdims=True)
        factor = jnp.where(row64[:, :1] > k, column / pivot, 0.0)
        m1[...] = whole - factor * one
        m2[...] = m2[...] - factor * two
        return carry

    lax.fori_loop(0, 32, eliminate, 0)
    step(CHUNKS + 4)
    lax.fori_loop(32, 64, eliminate, 0)
    diag = jnp.sum(jnp.where(lane64 == row64, m1[...], 0.0), axis=1, keepdims=True)
    scale = 1.0 / jnp.sqrt(diag)
    tri = m2[...] * scale
    proj = lax.dot_general(m1[...] * scale, tri, (((0,), (0,)), ((), ())),
                           precision=lax.Precision.HIGHEST, preferred_element_type=F32)
    row8 = lax.broadcasted_iota(jnp.int32, (8, ALL), 0)
    wanted = jnp.where(row8 < 4, row8, row8 + 28) + 4 * band
    pick = jnp.where(lanes((8, ALL)) == wanted, 1.0, 0.0).astype(F32)
    mine = jnp.dot(pick, tri, precision=lax.Precision.HIGHEST, preferred_element_type=F32)
    coef = jnp.concatenate([mine, -proj[64:96], jnp.zeros((8, 128), F32)], axis=0)
    high = coef.astype(BF16).astype(F32)
    mixed = jnp.where(lanes((48, 128)) < 64, high, coef - high).astype(BF16)
    lhs[...] = jnp.concatenate([mixed, mixed], axis=1)
    step(CHUNKS + 5)
    later(4)
    step(CHUNKS + 6)
    keep.wait()

    outs = []
    for c in range(CHUNKS):
        arrived(CHUNKS + c)

        def body(step, carry, c=c):
            j4 = CROWS * c + 4 * step
            rows = jnp.concatenate([hmat[pl.ds(j4 + p, ALL, stride=STEP), :] for p in range(4)], axis=1)
            high, low = split(rows)
            rhs = jnp.concatenate([high, high, low, low], axis=0)
            res = jnp.dot(lhs[...], rhs, preferred_element_type=F32)
            for p in range(4):
                piece = res[:, 128 * p:128 * p + 128]
                oblk2[pl.ds(j4 + p, 8, stride=STEP), :] = piece[:8]
                for g in range(4):
                    where = pl.ds(g * (8 * STEP) + j4 + p, 8, stride=STEP)
                    hacc[where, :] = hacc[where, :] + piece[8 + 8 * g:16 + 8 * g]
            return carry

        lax.fori_loop(0, CROWS // 4, body, 0)
        span = pl.ds(CROWS * c, CROWS)
        outs.append(pltpu.make_async_copy(oblk.at[:, :, span, :], hb_out.at[:, :, span, :], out_sem.at[0, c]))
        outs.append(pltpu.make_async_copy(hacc3.at[:, span, :], hl_out.at[:, span, :], out_sem.at[1, c]))
        outs[-2].start()
        outs[-1].start()

    halo_sent(range(10))
    passed(range(VIA, 10))
    for u in range(UNITS):
        for sid in range(7):
            move(u, sid).wait_send()
    for k in range(1, 16):
        scatter(k).wait_send()
        spread(k).wait_send()
    for copy in outs:
        copy.wait()


def rows_of(x):
    lead = x.shape[:-2]
    x = x.reshape(*lead, 4, 48, 128)
    return jnp.swapaxes(x, -3, -2).reshape(*lead, ROWS, 128)


def planes_of(x):
    lead = x.shape[:-2]
    x = jnp.swapaxes(x.reshape(*lead, 48, 4, 128), -3, -2)
    return x.reshape(*lead, 4, 48 * 128)


def local(blocks, later, potential):
    hb, hl = pl.pallas_call(
        kernel,
        out_shape=[jax.ShapeDtypeStruct((2, 4, ROWS, 128), F32), jax.ShapeDtypeStruct((NL, ROWS, 128), F32)],
        in_specs=[pl.BlockSpec(memory_space=pl.ANY), pl.BlockSpec(memory_space=pl.ANY),
                  pl.BlockSpec(memory_space=pltpu.VMEM)],
        out_specs=[pl.BlockSpec(memory_space=pl.ANY), pl.BlockSpec(memory_space=pl.ANY)],
        scratch_shapes=[
            pltpu.VMEM((2, 2, 32, STEP, 128), F32),
            pltpu.VMEM((41, PITCH, 128), F32),
            pltpu.VMEM((40, STEP, 128), F32),
            pltpu.VMEM((40, STEP, 128), F32),
            pltpu.VMEM((10 - VIA, 4, ROWS, 128), F32),
            pltpu.VMEM((2, 4, STEP, 128), F32),
            pltpu.VMEM((NL, STEP, 128), F32),
            pltpu.VMEM((2, 4, STEP, 128), F32),
            pltpu.VMEM((192, 128), F32),
            pltpu.VMEM((128, 128), F32),
            pltpu.VMEM((16, 8, 128), F32),
            pltpu.VMEM((8, 128), F32),
            pltpu.VMEM((128, 128), F32),
            pltpu.VMEM((ALL, 128), F32),
            pltpu.VMEM((ALL, 128), F32),
            pltpu.VMEM((48, 256), BF16),
            pltpu.SemaphoreType.DMA((5,)),
            pltpu.SemaphoreType.DMA((UNITS, 7)),
            pltpu.SemaphoreType.DMA((UNITS, 7)),
            pltpu.SemaphoreType.DMA((10, 2)),
            pltpu.SemaphoreType.DMA((10, 2)),
            pltpu.SemaphoreType.DMA((10 - VIA,)),
            pltpu.SemaphoreType.DMA((10 - VIA,)),
            pltpu.SemaphoreType.DMA((16,)),
            pltpu.SemaphoreType.DMA((16,)),
            pltpu.SemaphoreType.DMA((16,)),
            pltpu.SemaphoreType.DMA((16,)),
            pltpu.SemaphoreType.DMA((2, CHUNKS)),
        ],
        compiler_params=pltpu.CompilerParams(
            collective_id=0, has_side_effects=True, vmem_limit_bytes=56 * 1024 * 1024),
    )(rows_of(blocks), rows_of(later), rows_of(potential))
    return planes_of(hb), planes_of(hl)


def solution(mesh):
    return jax.shard_map(
        local,
        mesh=mesh,
        in_specs=(P(None, "band", "space", None), P("band", "space", None), P("space", None)),
        out_specs=(P(None, "band", "space", None), P("band", "space", None)),
        check_vma=False,
    )
```

```python
import functools

import jax
import jax.numpy as jnp
from jax import lax
from jax.experimental import pallas as pl
from jax.experimental.pallas import tpu as pltpu
from jax.sharding import PartitionSpec as P

MESH = pl.DeviceIdType.MESH
F32 = jnp.float32
BF16 = jnp.bfloat16
NZ = 96
ROWS = 192
PAD = 16
PITCH = 216
STEP = 200
CHUNKS = 6
CROWS = ROWS // CHUNKS
UNITS = 2 * CHUNKS
HALOS = {0: (0, 3), 1: (1,), 2: (2, 5), 4: (4, 7), 6: (6, 9), 8: (8,)}
PASSES = {2: (3,), 4: (5,), 6: (7,), 8: (9,)}
NB = 8
NL = 32
VIA = (3, 5, 7, 9)
ALL = 64
weights = (-205.0 / 72.0, 8.0 / 5.0, -1.0 / 5.0, 8.0 / 315.0, -1.0 / 560.0)


def lanes(shape=(8, 128)):
    return lax.broadcasted_iota(jnp.int32, shape, len(shape) - 1)


def split(value):
    high = value.astype(BF16)
    return high, (value - high.astype(F32)).astype(BF16)


def stencil(own, left, right, pot, group, out):
    ref, base = out
    lane = lanes()

    def load(chunk, plane):
        return own[pl.ds(group * (8 * PITCH) + PAD + 4 * chunk + plane, 8, stride=PITCH), :]

    def shifted(row, shift):
        q, e = shift // 128, shift % 128
        if e == 0:
            return row[q + 3]
        mixed = jnp.where(lane >= e, row[q + 3], row[q + 4])
        return pltpu.roll(mixed, 128 - e, 1)

    def one(chunk, third):
        zpos = lane + 32 * third
        zpos = jnp.where(zpos >= NZ, zpos - NZ, zpos)
        rows = [[load(chunk + d, plane) for d in range(-3, 4)] for plane in range(4)]
        halo = group * (8 * STEP) + 4 * chunk
        xs = [left[pl.ds(halo + plane, 8, stride=STEP), :] for plane in range(4)]
        xs += [rows[plane][3] for plane in range(4)]
        xs += [right[pl.ds(halo + plane, 8, stride=STEP), :] for plane in range(4)]
        for plane in range(4):
            row = rows[plane]
            acc = (pot[pl.ds(4 * chunk + plane, 1), :] - 1.5 * weights[0]) * row[3]
            for k in range(1, 5):
                part = xs[4 + plane + k] + xs[4 + plane - k]
                part = part + (shifted(row, NZ * k) + shifted(row, -NZ * k))
                up = jnp.where(zpos < NZ - k, shifted(row, k), 0.0)
                down = jnp.where(zpos >= k, shifted(row, -k), 0.0)
                acc = acc + (-0.5 * weights[k]) * (part + (up + down))
            ref[pl.ds(base + 4 * chunk + plane, 8, stride=STEP), :] = acc

    def body(step, carry):
        for third in range(3):
            one(3 * step + third, third)
        return carry

    lax.fori_loop(0, ROWS // 12, body, 0)


def kernel(blk, lat, pot, hb_out, hl_out,
           gath, own3, left3, right3, relay, hown, hacc3, oblk,
           acc, gs, rbuf, red, full, m1, m2, lhs,
           loc_sem, ag_send, ag_recv, halo_send, halo_recv, relay_send, relay_recv, rs_send, rs_recv, bc_send, bc_recv, out_sem):
    space = lax.axis_index("space")
    band = lax.axis_index("band")
    z, y = band // 4, band % 4

    def at(dy, dz):
        return lax.rem(z + dz, 2) * 4 + lax.rem(y + dy + 4, 4)

    own = own3.reshape(41 * PITCH, 128)
    left = left3.reshape(40 * STEP, 128)
    right = right3.reshape(40 * STEP, 128)
    hacc = hacc3.reshape(NL * STEP, 128)
    hown2 = hown.reshape(NB * STEP, 128)
    oblk2 = oblk.reshape(NB * STEP, 128)
    bmat = gath.at[0].reshape(ALL * STEP, 128)
    hmat = gath.at[1].reshape(ALL * STEP, 128)

    barrier = pltpu.get_barrier_semaphore()
    for b in (at(1, 0), at(-1, 0), at(0, 1)):
        pl.semaphore_signal(barrier, inc=1, device_id={"band": b}, device_id_type=MESH)

    half = space // 8 * 8
    turn = space - half

    @pl.loop(1, 8)
    def _(k):
        pl.semaphore_signal(barrier, inc=1, device_id={"space": half + lax.rem(turn + k, 8)}, device_id_type=MESH)

    opposite = lax.rem(space + 8, 16)
    pl.semaphore_signal(barrier, inc=1, device_id={"space": opposite}, device_id_type=MESH)
    pl.semaphore_signal(barrier, inc=1, device_id={"space": 15 - space}, device_id_type=MESH)

    local_copies = [
        pltpu.make_async_copy(blk.at[0], own3.at[pl.ds(0, 4), pl.ds(PAD, ROWS), :], loc_sem.at[0]),
        pltpu.make_async_copy(blk.at[1], own3.at[pl.ds(4, 4), pl.ds(PAD, ROWS), :], loc_sem.at[1]),
        pltpu.make_async_copy(lat, own3.at[pl.ds(8, NL), pl.ds(PAD, ROWS), :], loc_sem.at[2]),
        pltpu.make_async_copy(blk, gath.at[0, :, pl.ds(4 * band, 4), pl.ds(0, ROWS), :], loc_sem.at[3]),
    ]
    for copy in local_copies:
        copy.start()
    pl.semaphore_wait(barrier, 12)

    def source(part):
        return blk.at[part] if part < 2 else lat.at[pl.ds(4 * (part - 2), 4)]

    def halo(part, side):
        ref = left3 if side == 0 else right3
        return pltpu.make_async_remote_copy(
            src_ref=source(part), dst_ref=ref.at[pl.ds(4 * part, 4), pl.ds(0, ROWS), :],
            send_sem=halo_send.at[part, side], recv_sem=halo_recv.at[part, side],
            device_id={"space": space + 1 if side == 0 else space - 1}, device_id_type=MESH)

    def detour(part, side):
        return pltpu.make_async_remote_copy(
            src_ref=source(part), dst_ref=relay.at[VIA.index(part)],
            send_sem=halo_send.at[part, side], recv_sem=relay_recv.at[VIA.index(part)],
            device_id={"space": space + 8 if side == 0 else space - 8}, device_id_type=MESH)

    def onward(part, side):
        ref = left3 if side == 0 else right3
        return pltpu.make_async_remote_copy(
            src_ref=relay.at[VIA.index(part)], dst_ref=ref.at[pl.ds(4 * part, 4), pl.ds(0, ROWS), :],
            send_sem=relay_send.at[VIA.index(part)], recv_sem=halo_recv.at[part, side],
            device_id={"space": space - 7 if side == 0 else space + 7}, device_id_type=MESH)

    senders = ((space < 15, space == 7, space != 7), (space > 0, space == 8, space != 8))

    def halo_each(parts, direct, around):
        for side, (any_, seam, inner) in enumerate(senders):
            @pl.when(any_)
            def _(side=side):
                for part in parts:
                    if part not in VIA:
                        direct(part, side)

            if set(VIA) & set(parts):
                @pl.when(any_ & inner)
                def _(side=side):
                    for part in parts:
                        if part in VIA:
                            direct(part, side)

                @pl.when(seam)
                def _(side=side):
                    for part in parts:
                        if part in VIA:
                            around(part, side)

    def halo_start(parts):
        halo_each(parts, lambda p, s: halo(p, s).start(), lambda p, s: detour(p, s).start())

    def halo_sent(parts):
        halo_each(parts, lambda p, s: halo(p, s).wait_send(), lambda p, s: detour(p, s).wait_send())

    def halo_wait(parts):
        for side, there in enumerate((space > 0, space < 15)):
            @pl.when(there)
            def _(side=side):
                for part in parts:
                    halo(part, side).wait_recv()

    def pass_on(parts):
        for side, here in enumerate((space == 15, space == 0)):
            @pl.when(here)
            def _(side=side):
                for part in parts:
                    detour(part, side).wait_recv()
                    onward(part, side).start()

    def passed(parts):
        for side, here in enumerate((space == 15, space == 0)):
            @pl.when(here)
            def _(side=side):
                for part in parts:
                    onward(part, side).wait_send()

    def slot(u, b):
        return gath.at[u // CHUNKS, :, pl.ds(4 * b, 4), pl.ds(CROWS * (u % CHUNKS), CROWS), :]

    def move(u, sid):
        even = u % 2 == 0
        source, to = {
            0: ((0, 0), (1, 0)), 1: ((0, 0), (-1, 0)), 2: ((0, 0), (0, 1)),
            3: ((-1, 0), (1, 0)) if even else ((1, 0), (-1, 0)),
            4: ((0, 1), (1, 0)), 5: ((0, 1), (-1, 0)), 6: ((2, 0), (0, 1)),
        }[sid]
        place = slot(u, at(*source))
        if sid < 3:
            part = blk if u < CHUNKS else hown
            src = part.at[:, :, pl.ds(CROWS * (u % CHUNKS), CROWS), :]
        else:
            src = place
        return pltpu.make_async_remote_copy(
            src_ref=src, dst_ref=place, send_sem=ag_send.at[u, sid], recv_sem=ag_recv.at[u, sid],
            device_id={"band": at(*to)}, device_id_type=MESH)

    def start_own(u):
        for sid in (0, 1, 2):
            move(u, sid).start()

    def forward(u):
        move(u, 2).wait_recv()
        move(u, 4).start()
        move(u, 5).start()
        move(u, 0 if u % 2 == 0 else 1).wait_recv()
        move(u, 3).start()

    def across(u):
        move(u, 3).wait_recv()
        move(u, 6).start()

    def arrived(u):
        for sid in (1 if u % 2 == 0 else 0, 4, 5, 6):
            move(u, sid).wait_recv()

    def gram(c):
        def body(step, carry):
            j4 = CROWS * c + 4 * step
            rows = jnp.concatenate([
                jnp.concatenate([bmat[pl.ds(j4 + p, ALL, stride=STEP), :],
                                 own[pl.ds(8 * PITCH + PAD + j4 + p, NL, stride=PITCH), :]], axis=0)
                for p in range(4)], axis=1)
            high, low = split(rows)
            a = jnp.concatenate([high, low], axis=0)
            b = jnp.concatenate([high[:ALL], low[:ALL]], axis=0)
            acc[...] += lax.dot_general(a, b, (((1,), (1,)), ((), ())), preferred_element_type=F32)
            return carry

        lax.fori_loop(0, CROWS // 4, body, 0)

    start_own(0)
    start_own(1)
    for copy in local_copies:
        copy.wait()

    @pl.loop(0, 41)
    def _(o):
        own3[o, pl.ds(0, PAD), :] = jnp.zeros((PAD, 128), F32)
        own3[o, pl.ds(PAD + ROWS, 8), :] = jnp.zeros((8, 128), F32)

    @pl.when(space == 0)
    def _():
        left3[...] = jnp.zeros(left3.shape, F32)

    @pl.when(space == 15)
    def _():
        right3[...] = jnp.zeros(right3.shape, F32)

    acc[...] = jnp.zeros(acc.shape, F32)

    def later(g):
        halo_wait((2 * g, 2 * g + 1))
        stencil(own, left, right, pot, g, (hacc, (g - 1) * (8 * STEP)))

    def step(t):
        if t < UNITS:
            forward(t)
        if 1 <= t:
            across(t - 1)
        if t + 2 < UNITS:
            start_own(t + 2)
        halo_start(HALOS.get(t, ()))
        pass_on(PASSES.get(t, ()))

    for t in range(CHUNKS - 2):
        step(t)
        if t >= 2:
            arrived(t - 2)
            gram(t - 2)
        if t == CHUNKS - 3:
            halo_wait((0, 1))
            stencil(own, left, right, pot, 0, (hown2, 0))
            keep = pltpu.make_async_copy(hown.at[:, :, pl.ds(0, ROWS), :], gath.at[1, :, pl.ds(4 * band, 4), pl.ds(0, ROWS), :],
                                         loc_sem.at[4])
            keep.start()
    for t in range(CHUNKS - 2, CHUNKS + 2):
        step(t)
        if t == CHUNKS:
            later(1)
        arrived(t - 2)
        gram(t - 2)

    low64 = lanes((48, 128)) < 64
    both = acc[:96] + acc[96:]
    both = both + pltpu.roll(both, 64, 1)
    gs[...] = jnp.where(low64, both[:48], both[48:])

    def scatter(k):
        return pltpu.make_async_remote_copy(
            src_ref=gs, dst_ref=rbuf.at[turn], send_sem=rs_send.at[k], recv_sem=rs_recv.at[k],
            device_id={"space": half + lax.rem(turn + k, 8)}, device_id_type=MESH)

    cross = pltpu.make_async_remote_copy(
        src_ref=red, dst_ref=full, send_sem=bc_send.at[0], recv_sem=bc_recv.at[0],
        device_id={"space": opposite}, device_id_type=MESH)

    for k in range(1, 8):
        scatter(k).start()
    rbuf[pl.ds(turn, 1)] = gs[...][None]
    later(2)
    step(CHUNKS + 2)
    for k in range(1, 8):
        scatter(k).wait_recv()
    red[...] = jnp.sum(rbuf[...], axis=0)
    cross.start()
    later(3)
    step(CHUNKS + 3)
    cross.wait_recv()

    cells = 16.0 * ROWS * 128
    total = red[...] + full[...]
    total = jnp.concatenate([total, pltpu.roll(total, 64, 1), jnp.zeros((32, 128), F32)], axis=0)
    m1[...] = jnp.transpose(total)[:ALL] * (1.0 / cells)
    lane64 = lanes((ALL, 128))
    row64 = lax.broadcasted_iota(jnp.int32, (ALL, 128), 0)
    m2[...] = jnp.where((lane64 == row64) | (lane64 == row64 + ALL), 1.0, 0.0).astype(F32)
    lane1 = lanes((1, 128))

    def eliminate(k, carry):
        one, two = m1[pl.ds(k, 1), :], m2[pl.ds(k, 1), :]
        pivot = jnp.sum(jnp.where(lane1 == k, one, 0.0), axis=1, keepdims=True)
        whole = m1[...]
        column = jnp.sum(jnp.where(lane64 == k, whole, 0.0), axis=1, keepdims=True)
        factor = jnp.where(row64[:, :1] > k, column / pivot, 0.0)
        m1[...] = whole - factor * one
        m2[...] = m2[...] - factor * two
        return carry

    lax.fori_loop(0, 32, eliminate, 0)
    step(CHUNKS + 4)
    lax.fori_loop(32, 64, eliminate, 0)
    diag = jnp.sum(jnp.where(lane64 == row64, m1[...], 0.0), axis=1, keepdims=True)
    scale = 1.0 / jnp.sqrt(diag)
    tri = m2[...] * scale
    proj = lax.dot_general(m1[...] * scale, tri, (((0,), (0,)), ((), ())),
                           precision=lax.Precision.HIGHEST, preferred_element_type=F32)
    row8 = lax.broadcasted_iota(jnp.int32, (8, ALL), 0)
    wanted = jnp.where(row8 < 4, row8, row8 + 28) + 4 * band
    pick = jnp.where(lanes((8, ALL)) == wanted, 1.0, 0.0).astype(F32)
    mine = jnp.dot(pick, tri, precision=lax.Precision.HIGHEST, preferred_element_type=F32)
    coef = jnp.concatenate([mine, -proj[64:96], jnp.zeros((8, 128), F32)], axis=0)
    high = coef.astype(BF16).astype(F32)
    mixed = jnp.where(lanes((48, 128)) < 64, high, coef - high).astype(BF16)
    lhs[...] = jnp.concatenate([mixed, mixed], axis=1)
    step(CHUNKS + 5)
    later(4)
    step(CHUNKS + 6)
    keep.wait()

    outs = []
    for c in range(CHUNKS):
        arrived(CHUNKS + c)

        def body(step, carry, c=c):
            j4 = CROWS * c + 4 * step
            rows = jnp.concatenate([hmat[pl.ds(j4 + p, ALL, stride=STEP), :] for p in range(4)], axis=1)
            high, low = split(rows)
            rhs = jnp.concatenate([high, high, low, low], axis=0)
            res = jnp.dot(lhs[...], rhs, preferred_element_type=F32)
            for p in range(4):
                piece = res[:, 128 * p:128 * p + 128]
                oblk2[pl.ds(j4 + p, 8, stride=STEP), :] = piece[:8]
                for g in range(4):
                    where = pl.ds(g * (8 * STEP) + j4 + p, 8, stride=STEP)
                    hacc[where, :] = hacc[where, :] + piece[8 + 8 * g:16 + 8 * g]
            return carry

        lax.fori_loop(0, CROWS // 4, body, 0)
        span = pl.ds(CROWS * c, CROWS)
        outs.append(pltpu.make_async_copy(oblk.at[:, :, span, :], hb_out.at[:, :, span, :], out_sem.at[0, c]))
        outs.append(pltpu.make_async_copy(hacc3.at[:, span, :], hl_out.at[:, span, :], out_sem.at[1, c]))
        outs[-2].start()
        outs[-1].start()

    halo_sent(range(10))
    passed(VIA)
    for u in range(UNITS):
        for sid in range(7):
            move(u, sid).wait_send()
    for k in range(1, 8):
        scatter(k).wait_send()
    cross.wait_send()
    for copy in outs:
        copy.wait()


def hand_over(hb, hl, hb_out, hl_out, held, get, put):
    pairs = [(hb.at[i], hb_out.at[i]) for i in range(2)]
    pairs += [(hl.at[pl.ds(4 * i, 4)], hl_out.at[pl.ds(4 * i, 4)]) for i in range(NL // 4)]
    there = [pltpu.make_async_copy(src, held.at[i], get.at[i]) for i, (src, _) in enumerate(pairs)]
    back = [pltpu.make_async_copy(held.at[i], dst, put.at[i]) for i, (_, dst) in enumerate(pairs)]
    for copy in there:
        copy.start()
    for first, second in zip(there, back):
        first.wait()
        second.start()
    for copy in back:
        copy.wait()


def rows_of(x):
    lead = x.shape[:-2]
    x = x.reshape(*lead, 4, 48, 128)
    return jnp.swapaxes(x, -3, -2).reshape(*lead, ROWS, 128)


def planes_of(x):
    lead = x.shape[:-2]
    x = jnp.swapaxes(x.reshape(*lead, 48, 4, 128), -3, -2)
    return x.reshape(*lead, 4, 48 * 128)


def local(blocks, later, potential):
    hb, hl = pl.pallas_call(
        kernel,
        out_shape=[jax.ShapeDtypeStruct((2, 4, ROWS, 128), F32), jax.ShapeDtypeStruct((NL, ROWS, 128), F32)],
        in_specs=[pl.BlockSpec(memory_space=pl.ANY), pl.BlockSpec(memory_space=pl.ANY),
                  pl.BlockSpec(memory_space=pltpu.VMEM)],
        out_specs=[pl.BlockSpec(memory_space=pl.ANY), pl.BlockSpec(memory_space=pl.ANY)],
        scratch_shapes=[
            pltpu.VMEM((2, 2, 32, STEP, 128), F32),
            pltpu.VMEM((41, PITCH, 128), F32),
            pltpu.VMEM((40, STEP, 128), F32),
            pltpu.VMEM((40, STEP, 128), F32),
            pltpu.VMEM((len(VIA), 4, ROWS, 128), F32),
            pltpu.VMEM((2, 4, STEP, 128), F32),
            pltpu.VMEM((NL, STEP, 128), F32),
            pltpu.VMEM((2, 4, STEP, 128), F32),
            pltpu.VMEM((192, 128), F32),
            pltpu.VMEM((48, 128), F32),
            pltpu.VMEM((8, 48, 128), F32),
            pltpu.VMEM((48, 128), F32),
            pltpu.VMEM((48, 128), F32),
            pltpu.VMEM((ALL, 128), F32),
            pltpu.VMEM((ALL, 128), F32),
            pltpu.VMEM((48, 256), BF16),
            pltpu.SemaphoreType.DMA((5,)),
            pltpu.SemaphoreType.DMA((UNITS, 7)),
            pltpu.SemaphoreType.DMA((UNITS, 7)),
            pltpu.SemaphoreType.DMA((10, 2)),
            pltpu.SemaphoreType.DMA((10, 2)),
            pltpu.SemaphoreType.DMA((len(VIA),)),
            pltpu.SemaphoreType.DMA((len(VIA),)),
            pltpu.SemaphoreType.DMA((8,)),
            pltpu.SemaphoreType.DMA((8,)),
            pltpu.SemaphoreType.DMA((1,)),
            pltpu.SemaphoreType.DMA((1,)),
            pltpu.SemaphoreType.DMA((2, CHUNKS)),
        ],
        compiler_params=pltpu.CompilerParams(
            collective_id=0, has_side_effects=True, vmem_limit_bytes=56 * 1024 * 1024),
    )(rows_of(blocks), rows_of(later), rows_of(potential))
    count = 2 + NL // 4
    hb, hl = pl.pallas_call(
        hand_over,
        out_shape=[jax.ShapeDtypeStruct(hb.shape, F32), jax.ShapeDtypeStruct(hl.shape, F32)],
        in_specs=[pl.BlockSpec(memory_space=pl.ANY)] * 2,
        out_specs=[pl.BlockSpec(memory_space=pl.ANY)] * 2,
        scratch_shapes=[pltpu.VMEM((count, 4, ROWS, 128), F32), pltpu.SemaphoreType.DMA((count,)),
                        pltpu.SemaphoreType.DMA((count,))],
        compiler_params=pltpu.CompilerParams(vmem_limit_bytes=56 * 1024 * 1024),
    )(hb, hl)
    return planes_of(hb), planes_of(hl)


def solution(mesh):
    return jax.shard_map(
        local,
        mesh=mesh,
        in_specs=(P(None, "band", "space", None), P("band", "space", None), P("space", None)),
        out_specs=(P(None, "band", "space", None), P("band", "space", None)),
        check_vma=False,
    )
```

```python
import functools

import jax
import jax.numpy as jnp
from jax import lax
from jax.experimental import pallas as pl
from jax.experimental.pallas import tpu as pltpu
from jax.sharding import PartitionSpec as P

MESH = pl.DeviceIdType.MESH
F32 = jnp.float32
BF16 = jnp.bfloat16
NZ = 96
ROWS = 192
PAD = 16
PITCH = 216
STEP = 200
CHUNKS = 6
CROWS = ROWS // CHUNKS
UNITS = 2 * CHUNKS
HALOS = {0: (0, 3), 1: (1,), 2: (2, 5), 4: (4, 7), 6: (6, 9), 8: (8,)}
PASSES = {2: (3,), 4: (5,), 6: (7,), 8: (9,)}
NB = 8
NL = 32
VIA = (3, 5, 7, 9)
ALL = 64
weights = (-205.0 / 72.0, 8.0 / 5.0, -1.0 / 5.0, 8.0 / 315.0, -1.0 / 560.0)


def lanes(shape=(8, 128)):
    return lax.broadcasted_iota(jnp.int32, shape, len(shape) - 1)


def split(value):
    high = value.astype(BF16)
    return high, (value - high.astype(F32)).astype(BF16)


def stencil(own, left, right, pot, group, out):
    ref, base = out
    lane = lanes()

    def load(chunk, plane):
        return own[pl.ds(group * (8 * PITCH) + PAD + 4 * chunk + plane, 8, stride=PITCH), :]

    def shifted(row, shift):
        q, e = shift // 128, shift % 128
        if e == 0:
            return row[q + 3]
        mixed = jnp.where(lane >= e, row[q + 3], row[q + 4])
        return pltpu.roll(mixed, 128 - e, 1)

    def one(chunk, third):
        zpos = lane + 32 * third
        zpos = jnp.where(zpos >= NZ, zpos - NZ, zpos)
        rows = [[load(chunk + d, plane) for d in range(-3, 4)] for plane in range(4)]
        halo = group * (8 * STEP) + 4 * chunk
        xs = [left[pl.ds(halo + plane, 8, stride=STEP), :] for plane in range(4)]
        xs += [rows[plane][3] for plane in range(4)]
        xs += [right[pl.ds(halo + plane, 8, stride=STEP), :] for plane in range(4)]
        for plane in range(4):
            row = rows[plane]
            acc = (pot[pl.ds(4 * chunk + plane, 1), :] - 1.5 * weights[0]) * row[3]
            for k in range(1, 5):
                part = xs[4 + plane + k] + xs[4 + plane - k]
                part = part + (shifted(row, NZ * k) + shifted(row, -NZ * k))
                up = jnp.where(zpos < NZ - k, shifted(row, k), 0.0)
                down = jnp.where(zpos >= k, shifted(row, -k), 0.0)
                acc = acc + (-0.5 * weights[k]) * (part + (up + down))
            ref[pl.ds(base + 4 * chunk + plane, 8, stride=STEP), :] = acc

    def body(step, carry):
        for third in range(3):
            one(3 * step + third, third)
        return carry

    lax.fori_loop(0, ROWS // 12, body, 0)


def kernel(blk, lat, pot, hb_out, hl_out,
           gath, own3, left3, right3, relay, hown, hacc3, oblk,
           acc, gs, rbuf, red, full, m1, m2, lhs,
           loc_sem, ag_send, ag_recv, halo_send, halo_recv, relay_send, relay_recv, rs_send, rs_recv, bc_send, bc_recv, out_sem):
    space = lax.axis_index("space")
    band = lax.axis_index("band")
    z, y = band // 4, band % 4

    def at(dy, dz):
        return lax.rem(z + dz, 2) * 4 + lax.rem(y + dy + 4, 4)

    own = own3.reshape(41 * PITCH, 128)
    left = left3.reshape(40 * STEP, 128)
    right = right3.reshape(40 * STEP, 128)
    hacc = hacc3.reshape(NL * STEP, 128)
    hown2 = hown.reshape(NB * STEP, 128)
    oblk2 = oblk.reshape(NB * STEP, 128)
    bmat = gath.at[0].reshape(ALL * STEP, 128)
    hmat = gath.at[1].reshape(ALL * STEP, 128)

    barrier = pltpu.get_barrier_semaphore()
    for b in (at(1, 0), at(-1, 0), at(0, 1)):
        pl.semaphore_signal(barrier, inc=1, device_id={"band": b}, device_id_type=MESH)

    half = space // 8 * 8
    turn = space - half

    @pl.loop(1, 8)
    def _(k):
        pl.semaphore_signal(barrier, inc=1, device_id={"space": half + lax.rem(turn + k, 8)}, device_id_type=MESH)

    opposite = lax.rem(space + 8, 16)
    pl.semaphore_signal(barrier, inc=1, device_id={"space": opposite}, device_id_type=MESH)
    pl.semaphore_signal(barrier, inc=1, device_id={"space": 15 - space}, device_id_type=MESH)

    local_copies = [
        pltpu.make_async_copy(blk.at[0], own3.at[pl.ds(0, 4), pl.ds(PAD, ROWS), :], loc_sem.at[0]),
        pltpu.make_async_copy(blk.at[1], own3.at[pl.ds(4, 4), pl.ds(PAD, ROWS), :], loc_sem.at[1]),
        pltpu.make_async_copy(lat, own3.at[pl.ds(8, NL), pl.ds(PAD, ROWS), :], loc_sem.at[2]),
        pltpu.make_async_copy(blk, gath.at[0, :, pl.ds(4 * band, 4), pl.ds(0, ROWS), :], loc_sem.at[3]),
    ]
    for copy in local_copies:
        copy.start()
    pl.semaphore_wait(barrier, 12)

    def source(part):
        return blk.at[part] if part < 2 else lat.at[pl.ds(4 * (part - 2), 4)]

    def halo(part, side):
        ref = left3 if side == 0 else right3
        return pltpu.make_async_remote_copy(
            src_ref=source(part), dst_ref=ref.at[pl.ds(4 * part, 4), pl.ds(0, ROWS), :],
            send_sem=halo_send.at[part, side], recv_sem=halo_recv.at[part, side],
            device_id={"space": space + 1 if side == 0 else space - 1}, device_id_type=MESH)

    def detour(part, side):
        return pltpu.make_async_remote_copy(
            src_ref=source(part), dst_ref=relay.at[VIA.index(part)],
            send_sem=halo_send.at[part, side], recv_sem=relay_recv.at[VIA.index(part)],
            device_id={"space": space + 8 if side == 0 else space - 8}, device_id_type=MESH)

    def onward(part, side):
        ref = left3 if side == 0 else right3
        return pltpu.make_async_remote_copy(
            src_ref=relay.at[VIA.index(part)], dst_ref=ref.at[pl.ds(4 * part, 4), pl.ds(0, ROWS), :],
            send_sem=relay_send.at[VIA.index(part)], recv_sem=halo_recv.at[part, side],
            device_id={"space": space - 7 if side == 0 else space + 7}, device_id_type=MESH)

    senders = ((space < 15, space == 7, space != 7), (space > 0, space == 8, space != 8))

    def halo_each(parts, direct, around):
        for side, (any_, seam, inner) in enumerate(senders):
            @pl.when(any_)
            def _(side=side):
                for part in parts:
                    if part not in VIA:
                        direct(part, side)

            if set(VIA) & set(parts):
                @pl.when(any_ & inner)
                def _(side=side):
                    for part in parts:
                        if part in VIA:
                            direct(part, side)

                @pl.when(seam)
                def _(side=side):
                    for part in parts:
                        if part in VIA:
                            around(part, side)

    def halo_start(parts):
        halo_each(parts, lambda p, s: halo(p, s).start(), lambda p, s: detour(p, s).start())

    def halo_sent(parts):
        halo_each(parts, lambda p, s: halo(p, s).wait_send(), lambda p, s: detour(p, s).wait_send())

    def halo_wait(parts):
        for side, there in enumerate((space > 0, space < 15)):
            @pl.when(there)
            def _(side=side):
                for part in parts:
                    halo(part, side).wait_recv()

    def pass_on(parts):
        for side, here in enumerate((space == 15, space == 0)):
            @pl.when(here)
            def _(side=side):
                for part in parts:
                    detour(part, side).wait_recv()
                    onward(part, side).start()

    def passed(parts):
        for side, here in enumerate((space == 15, space == 0)):
            @pl.when(here)
            def _(side=side):
                for part in parts:
                    onward(part, side).wait_send()

    def slot(u, b):
        return gath.at[u // CHUNKS, :, pl.ds(4 * b, 4), pl.ds(CROWS * (u % CHUNKS), CROWS), :]

    def move(u, sid):
        even = u % 2 == 0
        source, to = {
            0: ((0, 0), (1, 0)), 1: ((0, 0), (-1, 0)), 2: ((0, 0), (0, 1)),
            3: ((-1, 0), (1, 0)) if even else ((1, 0), (-1, 0)),
            4: ((0, 1), (1, 0)), 5: ((0, 1), (-1, 0)), 6: ((2, 0), (0, 1)),
        }[sid]
        place = slot(u, at(*source))
        if sid < 3:
            part = blk if u < CHUNKS else hown
            src = part.at[:, :, pl.ds(CROWS * (u % CHUNKS), CROWS), :]
        else:
            src = place
        return pltpu.make_async_remote_copy(
            src_ref=src, dst_ref=place, send_sem=ag_send.at[u, sid], recv_sem=ag_recv.at[u, sid],
            device_id={"band": at(*to)}, device_id_type=MESH)

    def start_own(u):
        for sid in (0, 1, 2):
            move(u, sid).start()

    def forward(u):
        move(u, 0 if u % 2 == 0 else 1).wait_recv()
        move(u, 3).start()
        move(u, 2).wait_recv()
        move(u, 4).start()
        move(u, 5).start()

    def across(u):
        move(u, 3).wait_recv()
        move(u, 6).start()

    def arrived(u):
        for sid in (1 if u % 2 == 0 else 0, 4, 5, 6):
            move(u, sid).wait_recv()

    def gram(c):
        def body(step, carry):
            j4 = CROWS * c + 4 * step
            rows = jnp.concatenate([
                jnp.concatenate([bmat[pl.ds(j4 + p, ALL, stride=STEP), :],
                                 own[pl.ds(8 * PITCH + PAD + j4 + p, NL, stride=PITCH), :]], axis=0)
                for p in range(4)], axis=1)
            high, low = split(rows)
            a = jnp.concatenate([high, low], axis=0)
            b = jnp.concatenate([high[:ALL], low[:ALL]], axis=0)
            acc[...] += lax.dot_general(a, b, (((1,), (1,)), ((), ())), preferred_element_type=F32)
            return carry

        lax.fori_loop(0, CROWS // 4, body, 0)

    start_own(0)
    start_own(1)
    for copy in local_copies:
        copy.wait()

    @pl.loop(0, 41)
    def _(o):
        own3[o, pl.ds(0, PAD), :] = jnp.zeros((PAD, 128), F32)
        own3[o, pl.ds(PAD + ROWS, 8), :] = jnp.zeros((8, 128), F32)

    @pl.when(space == 0)
    def _():
        left3[...] = jnp.zeros(left3.shape, F32)

    @pl.when(space == 15)
    def _():
        right3[...] = jnp.zeros(right3.shape, F32)

    acc[...] = jnp.zeros(acc.shape, F32)

    def later(g):
        halo_wait((2 * g, 2 * g + 1))
        stencil(own, left, right, pot, g, (hacc, (g - 1) * (8 * STEP)))

    def step(t):
        if t < UNITS:
            forward(t)
        if 1 <= t:
            across(t - 1)
        if t + 2 < UNITS:
            start_own(t + 2)
        halo_start(HALOS.get(t, ()))
        pass_on(PASSES.get(t, ()))

    for t in range(CHUNKS - 2):
        step(t)
        if t >= 2:
            arrived(t - 2)
            gram(t - 2)
        if t == CHUNKS - 3:
            halo_wait((0, 1))
            stencil(own, left, right, pot, 0, (hown2, 0))
            keep = pltpu.make_async_copy(hown.at[:, :, pl.ds(0, ROWS), :], gath.at[1, :, pl.ds(4 * band, 4), pl.ds(0, ROWS), :],
                                         loc_sem.at[4])
            keep.start()
    for t in range(CHUNKS - 2, CHUNKS + 2):
        step(t)
        if t == CHUNKS:
            later(1)
        arrived(t - 2)
        gram(t - 2)

    low64 = lanes((48, 128)) < 64
    both = acc[:96] + acc[96:]
    both = both + pltpu.roll(both, 64, 1)
    gs[...] = jnp.where(low64, both[:48], both[48:])

    def scatter(k):
        return pltpu.make_async_remote_copy(
            src_ref=gs, dst_ref=rbuf.at[turn], send_sem=rs_send.at[k], recv_sem=rs_recv.at[k],
            device_id={"space": half + lax.rem(turn + k, 8)}, device_id_type=MESH)

    cross = pltpu.make_async_remote_copy(
        src_ref=red, dst_ref=full, send_sem=bc_send.at[0], recv_sem=bc_recv.at[0],
        device_id={"space": opposite}, device_id_type=MESH)

    for k in range(1, 8):
        scatter(k).start()
    rbuf[pl.ds(turn, 1)] = gs[...][None]
    later(2)
    step(CHUNKS + 2)
    for k in range(1, 8):
        scatter(k).wait_recv()
    red[...] = jnp.sum(rbuf[...], axis=0)
    cross.start()
    later(3)
    step(CHUNKS + 3)
    cross.wait_recv()

    cells = 16.0 * ROWS * 128
    total = red[...] + full[...]
    total = jnp.concatenate([total, pltpu.roll(total, 64, 1), jnp.zeros((32, 128), F32)], axis=0)
    m1[...] = jnp.transpose(total)[:ALL] * (1.0 / cells)
    lane64 = lanes((ALL, 128))
    row64 = lax.broadcasted_iota(jnp.int32, (ALL, 128), 0)
    m2[...] = jnp.where((lane64 == row64) | (lane64 == row64 + ALL), 1.0, 0.0).astype(F32)
    lane1 = lanes((1, 128))

    def eliminate(k, carry):
        one, two = m1[pl.ds(k, 1), :], m2[pl.ds(k, 1), :]
        pivot = jnp.sum(jnp.where(lane1 == k, one, 0.0), axis=1, keepdims=True)
        whole = m1[...]
        column = jnp.sum(jnp.where(lane64 == k, whole, 0.0), axis=1, keepdims=True)
        factor = jnp.where(row64[:, :1] > k, column / pivot, 0.0)
        m1[...] = whole - factor * one
        m2[...] = m2[...] - factor * two
        return carry

    lax.fori_loop(0, 32, eliminate, 0)
    step(CHUNKS + 4)
    lax.fori_loop(32, 64, eliminate, 0)
    diag = jnp.sum(jnp.where(lane64 == row64, m1[...], 0.0), axis=1, keepdims=True)
    scale = 1.0 / jnp.sqrt(diag)
    tri = m2[...] * scale
    proj = lax.dot_general(m1[...] * scale, tri, (((0,), (0,)), ((), ())),
                           precision=lax.Precision.HIGHEST, preferred_element_type=F32)
    row8 = lax.broadcasted_iota(jnp.int32, (8, ALL), 0)
    wanted = jnp.where(row8 < 4, row8, row8 + 28) + 4 * band
    pick = jnp.where(lanes((8, ALL)) == wanted, 1.0, 0.0).astype(F32)
    mine = jnp.dot(pick, tri, precision=lax.Precision.HIGHEST, preferred_element_type=F32)
    coef = jnp.concatenate([mine, -proj[64:96], jnp.zeros((8, 128), F32)], axis=0)
    high = coef.astype(BF16).astype(F32)
    mixed = jnp.where(lanes((48, 128)) < 64, high, coef - high).astype(BF16)
    lhs[...] = jnp.concatenate([mixed, mixed], axis=1)
    step(CHUNKS + 5)
    later(4)
    step(CHUNKS + 6)
    keep.wait()

    outs = []
    for c in range(CHUNKS):
        arrived(CHUNKS + c)

        def body(step, carry, c=c):
            j4 = CROWS * c + 4 * step
            rows = jnp.concatenate([hmat[pl.ds(j4 + p, ALL, stride=STEP), :] for p in range(4)], axis=1)
            high, low = split(rows)
            rhs = jnp.concatenate([high, high, low, low], axis=0)
            res = jnp.dot(lhs[...], rhs, preferred_element_type=F32)
            for p in range(4):
                piece = res[:, 128 * p:128 * p + 128]
                oblk2[pl.ds(j4 + p, 8, stride=STEP), :] = piece[:8]
                for g in range(4):
                    where = pl.ds(g * (8 * STEP) + j4 + p, 8, stride=STEP)
                    hacc[where, :] = hacc[where, :] + piece[8 + 8 * g:16 + 8 * g]
            return carry

        lax.fori_loop(0, CROWS // 4, body, 0)
        span = pl.ds(CROWS * c, CROWS)
        outs.append(pltpu.make_async_copy(oblk.at[:, :, span, :], hb_out.at[:, :, span, :], out_sem.at[0, c]))
        outs.append(pltpu.make_async_copy(hacc3.at[:, span, :], hl_out.at[:, span, :], out_sem.at[1, c]))
        outs[-2].start()
        outs[-1].start()

    halo_sent(range(10))
    passed(VIA)
    for u in range(UNITS):
        for sid in range(7):
            move(u, sid).wait_send()
    for k in range(1, 8):
        scatter(k).wait_send()
    cross.wait_send()
    for copy in outs:
        copy.wait()


def hand_over(hb, hl, hb_out, hl_out, held, get, put):
    pairs = [(hb.at[i], hb_out.at[i]) for i in range(2)]
    pairs += [(hl.at[pl.ds(4 * i, 4)], hl_out.at[pl.ds(4 * i, 4)]) for i in range(NL // 4)]
    there = [pltpu.make_async_copy(src, held.at[i], get.at[i]) for i, (src, _) in enumerate(pairs)]
    back = [pltpu.make_async_copy(held.at[i], dst, put.at[i]) for i, (_, dst) in enumerate(pairs)]
    for copy in there:
        copy.start()
    for first, second in zip(there, back):
        first.wait()
        second.start()
    for copy in back:
        copy.wait()


def rows_of(x):
    lead = x.shape[:-2]
    x = x.reshape(*lead, 4, 48, 128)
    return jnp.swapaxes(x, -3, -2).reshape(*lead, ROWS, 128)


def planes_of(x):
    lead = x.shape[:-2]
    x = jnp.swapaxes(x.reshape(*lead, 48, 4, 128), -3, -2)
    return x.reshape(*lead, 4, 48 * 128)


def local(blocks, later, potential):
    hb, hl = pl.pallas_call(
        kernel,
        out_shape=[jax.ShapeDtypeStruct((2, 4, ROWS, 128), F32), jax.ShapeDtypeStruct((NL, ROWS, 128), F32)],
        in_specs=[pl.BlockSpec(memory_space=pl.ANY), pl.BlockSpec(memory_space=pl.ANY),
                  pl.BlockSpec(memory_space=pltpu.VMEM)],
        out_specs=[pl.BlockSpec(memory_space=pl.ANY), pl.BlockSpec(memory_space=pl.ANY)],
        scratch_shapes=[
            pltpu.VMEM((2, 2, 32, STEP, 128), F32),
            pltpu.VMEM((41, PITCH, 128), F32),
            pltpu.VMEM((40, STEP, 128), F32),
            pltpu.VMEM((40, STEP, 128), F32),
            pltpu.VMEM((len(VIA), 4, ROWS, 128), F32),
            pltpu.VMEM((2, 4, STEP, 128), F32),
            pltpu.VMEM((NL, STEP, 128), F32),
            pltpu.VMEM((2, 4, STEP, 128), F32),
            pltpu.VMEM((192, 128), F32),
            pltpu.VMEM((48, 128), F32),
            pltpu.VMEM((8, 48, 128), F32),
            pltpu.VMEM((48, 128), F32),
            pltpu.VMEM((48, 128), F32),
            pltpu.VMEM((ALL, 128), F32),
            pltpu.VMEM((ALL, 128), F32),
            pltpu.VMEM((48, 256), BF16),
            pltpu.SemaphoreType.DMA((5,)),
            pltpu.SemaphoreType.DMA((UNITS, 7)),
            pltpu.SemaphoreType.DMA((UNITS, 7)),
            pltpu.SemaphoreType.DMA((10, 2)),
            pltpu.SemaphoreType.DMA((10, 2)),
            pltpu.SemaphoreType.DMA((len(VIA),)),
            pltpu.SemaphoreType.DMA((len(VIA),)),
            pltpu.SemaphoreType.DMA((8,)),
            pltpu.SemaphoreType.DMA((8,)),
            pltpu.SemaphoreType.DMA((1,)),
            pltpu.SemaphoreType.DMA((1,)),
            pltpu.SemaphoreType.DMA((2, CHUNKS)),
        ],
        compiler_params=pltpu.CompilerParams(
            collective_id=0, has_side_effects=True, vmem_limit_bytes=56 * 1024 * 1024),
    )(rows_of(blocks), rows_of(later), rows_of(potential))
    count = 2 + NL // 4
    hb, hl = pl.pallas_call(
        hand_over,
        out_shape=[jax.ShapeDtypeStruct(hb.shape, F32), jax.ShapeDtypeStruct(hl.shape, F32)],
        in_specs=[pl.BlockSpec(memory_space=pl.ANY)] * 2,
        out_specs=[pl.BlockSpec(memory_space=pl.ANY)] * 2,
        scratch_shapes=[pltpu.VMEM((count, 4, ROWS, 128), F32), pltpu.SemaphoreType.DMA((count,)),
                        pltpu.SemaphoreType.DMA((count,))],
        compiler_params=pltpu.CompilerParams(vmem_limit_bytes=56 * 1024 * 1024),
    )(hb, hl)
    return planes_of(hb), planes_of(hl)


def solution(mesh):
    return jax.shard_map(
        local,
        mesh=mesh,
        in_specs=(P(None, "band", "space", None), P("band", "space", None), P("space", None)),
        out_specs=(P(None, "band", "space", None), P("band", "space", None)),
        check_vma=False,
    )
```

```python
import functools

import jax
import jax.numpy as jnp
from jax import lax
from jax.experimental import pallas as pl
from jax.experimental.pallas import tpu as pltpu
from jax.sharding import PartitionSpec as P

MESH = pl.DeviceIdType.MESH
F32 = jnp.float32
BF16 = jnp.bfloat16
NZ = 96
ROWS = 192
PAD = 16
PITCH = 216
STEP = 200
CHUNKS = 6
CROWS = ROWS // CHUNKS
UNITS = 2 * CHUNKS
HALOS = {0: (0, 3), 1: (1,), 2: (2, 5), 4: (4, 7), 6: (6, 9), 8: (8,)}
PASSES = {2: (3,), 4: (5,), 6: (7,), 8: (9,)}
NB = 8
NL = 32
VIA = (3, 5, 7, 9)
ALL = 64
weights = (-205.0 / 72.0, 8.0 / 5.0, -1.0 / 5.0, 8.0 / 315.0, -1.0 / 560.0)


def lanes(shape=(8, 128)):
    return lax.broadcasted_iota(jnp.int32, shape, len(shape) - 1)


def split(value):
    high = value.astype(BF16)
    return high, (value - high.astype(F32)).astype(BF16)


def stencil(own, left, right, pot, group, out):
    ref, base = out
    lane = lanes()

    def load(chunk, plane):
        return own[pl.ds(group * (8 * PITCH) + PAD + 4 * chunk + plane, 8, stride=PITCH), :]

    def shifted(row, shift):
        q, e = shift // 128, shift % 128
        if e == 0:
            return row[q + 3]
        mixed = jnp.where(lane >= e, row[q + 3], row[q + 4])
        return pltpu.roll(mixed, 128 - e, 1)

    def one(chunk, third):
        zpos = lane + 32 * third
        zpos = jnp.where(zpos >= NZ, zpos - NZ, zpos)
        rows = [[load(chunk + d, plane) for d in range(-3, 4)] for plane in range(4)]
        halo = group * (8 * STEP) + 4 * chunk
        xs = [left[pl.ds(halo + plane, 8, stride=STEP), :] for plane in range(4)]
        xs += [rows[plane][3] for plane in range(4)]
        xs += [right[pl.ds(halo + plane, 8, stride=STEP), :] for plane in range(4)]
        for plane in range(4):
            row = rows[plane]
            acc = (pot[pl.ds(4 * chunk + plane, 1), :] - 1.5 * weights[0]) * row[3]
            for k in range(1, 5):
                part = xs[4 + plane + k] + xs[4 + plane - k]
                part = part + (shifted(row, NZ * k) + shifted(row, -NZ * k))
                up = jnp.where(zpos < NZ - k, shifted(row, k), 0.0)
                down = jnp.where(zpos >= k, shifted(row, -k), 0.0)
                acc = acc + (-0.5 * weights[k]) * (part + (up + down))
            ref[pl.ds(base + 4 * chunk + plane, 8, stride=STEP), :] = acc

    def body(step, carry):
        for third in range(3):
            one(3 * step + third, third)
        return carry

    lax.fori_loop(0, ROWS // 12, body, 0)


def kernel(blk, lat, pot, hb_out, hl_out,
           gath, own3, left3, right3, relay, hown, hacc3, oblk,
           acc, gs, rbuf, red, full, m1, m2, lhs,
           loc_sem, ag_send, ag_recv, halo_send, halo_recv, relay_send, relay_recv, rs_send, rs_recv, bc_send, bc_recv, out_sem):
    space = lax.axis_index("space")
    band = lax.axis_index("band")
    z, y = band // 4, band % 4

    def at(dy, dz):
        return lax.rem(z + dz, 2) * 4 + lax.rem(y + dy + 4, 4)

    own = own3.reshape(41 * PITCH, 128)
    left = left3.reshape(40 * STEP, 128)
    right = right3.reshape(40 * STEP, 128)
    hacc = hacc3.reshape(NL * STEP, 128)
    hown2 = hown.reshape(NB * STEP, 128)
    oblk2 = oblk.reshape(NB * STEP, 128)
    bmat = gath.at[0].reshape(ALL * STEP, 128)
    hmat = gath.at[1].reshape(ALL * STEP, 128)

    barrier = pltpu.get_barrier_semaphore()
    for b in (at(1, 0), at(-1, 0), at(0, 1)):
        pl.semaphore_signal(barrier, inc=1, device_id={"band": b}, device_id_type=MESH)

    half = space // 8 * 8
    turn = space - half

    @pl.loop(1, 8)
    def _(k):
        pl.semaphore_signal(barrier, inc=1, device_id={"space": half + lax.rem(turn + k, 8)}, device_id_type=MESH)

    opposite = lax.rem(space + 8, 16)
    pl.semaphore_signal(barrier, inc=1, device_id={"space": opposite}, device_id_type=MESH)
    pl.semaphore_signal(barrier, inc=1, device_id={"space": 15 - space}, device_id_type=MESH)

    local_copies = [
        pltpu.make_async_copy(blk.at[0], own3.at[pl.ds(0, 4), pl.ds(PAD, ROWS), :], loc_sem.at[0]),
        pltpu.make_async_copy(blk.at[1], own3.at[pl.ds(4, 4), pl.ds(PAD, ROWS), :], loc_sem.at[1]),
        pltpu.make_async_copy(lat, own3.at[pl.ds(8, NL), pl.ds(PAD, ROWS), :], loc_sem.at[2]),
        pltpu.make_async_copy(blk, gath.at[0, :, pl.ds(4 * band, 4), pl.ds(0, ROWS), :], loc_sem.at[3]),
    ]
    for copy in local_copies:
        copy.start()
    pl.semaphore_wait(barrier, 12)

    def source(part):
        return blk.at[part] if part < 2 else lat.at[pl.ds(4 * (part - 2), 4)]

    def halo(part, side):
        ref = left3 if side == 0 else right3
        return pltpu.make_async_remote_copy(
            src_ref=source(part), dst_ref=ref.at[pl.ds(4 * part, 4), pl.ds(0, ROWS), :],
            send_sem=halo_send.at[part, side], recv_sem=halo_recv.at[part, side],
            device_id={"space": space + 1 if side == 0 else space - 1}, device_id_type=MESH)

    def detour(part, side):
        return pltpu.make_async_remote_copy(
            src_ref=source(part), dst_ref=relay.at[VIA.index(part)],
            send_sem=halo_send.at[part, side], recv_sem=relay_recv.at[VIA.index(part)],
            device_id={"space": space + 8 if side == 0 else space - 8}, device_id_type=MESH)

    def onward(part, side):
        ref = left3 if side == 0 else right3
        return pltpu.make_async_remote_copy(
            src_ref=relay.at[VIA.index(part)], dst_ref=ref.at[pl.ds(4 * part, 4), pl.ds(0, ROWS), :],
            send_sem=relay_send.at[VIA.index(part)], recv_sem=halo_recv.at[part, side],
            device_id={"space": space - 7 if side == 0 else space + 7}, device_id_type=MESH)

    senders = ((space < 15, space == 7, space != 7), (space > 0, space == 8, space != 8))

    def halo_each(parts, direct, around):
        for side, (any_, seam, inner) in enumerate(senders):
            @pl.when(any_)
            def _(side=side):
                for part in parts:
                    if part not in VIA:
                        direct(part, side)

            if set(VIA) & set(parts):
                @pl.when(any_ & inner)
                def _(side=side):
                    for part in parts:
                        if part in VIA:
                            direct(part, side)

                @pl.when(seam)
                def _(side=side):
                    for part in parts:
                        if part in VIA:
                            around(part, side)

    def halo_start(parts):
        halo_each(parts, lambda p, s: halo(p, s).start(), lambda p, s: detour(p, s).start())

    def halo_sent(parts):
        halo_each(parts, lambda p, s: halo(p, s).wait_send(), lambda p, s: detour(p, s).wait_send())

    def halo_wait(parts):
        for side, there in enumerate((space > 0, space < 15)):
            @pl.when(there)
            def _(side=side):
                for part in parts:
                    halo(part, side).wait_recv()

    def pass_on(parts):
        for side, here in enumerate((space == 15, space == 0)):
            @pl.when(here)
            def _(side=side):
                for part in parts:
                    detour(part, side).wait_recv()
                    onward(part, side).start()

    def passed(parts):
        for side, here in enumerate((space == 15, space == 0)):
            @pl.when(here)
            def _(side=side):
                for part in parts:
                    onward(part, side).wait_send()

    def slot(u, b):
        return gath.at[u // CHUNKS, :, pl.ds(4 * b, 4), pl.ds(CROWS * (u % CHUNKS), CROWS), :]

    def move(u, sid):
        even = u % 2 == 0
        source, to = {
            0: ((0, 0), (1, 0)), 1: ((0, 0), (-1, 0)), 2: ((0, 0), (0, 1)),
            3: ((-1, 0), (1, 0)) if even else ((1, 0), (-1, 0)),
            4: ((0, 1), (1, 0)), 5: ((0, 1), (-1, 0)), 6: ((2, 0), (0, 1)),
        }[sid]
        place = slot(u, at(*source))
        if sid < 3:
            part = blk if u < CHUNKS else hown
            src = part.at[:, :, pl.ds(CROWS * (u % CHUNKS), CROWS), :]
        else:
            src = place
        return pltpu.make_async_remote_copy(
            src_ref=src, dst_ref=place, send_sem=ag_send.at[u, sid], recv_sem=ag_recv.at[u, sid],
            device_id={"band": at(*to)}, device_id_type=MESH)

    def start_own(u):
        for sid in (0, 1, 2):
            move(u, sid).start()

    def forward(u):
        move(u, 0 if u % 2 == 0 else 1).wait_recv()
        move(u, 3).start()
        move(u, 2).wait_recv()
        move(u, 4).start()
        move(u, 5).start()

    def across(u):
        move(u, 3).wait_recv()
        move(u, 6).start()

    def arrived(u):
        for sid in (1 if u % 2 == 0 else 0, 4, 5, 6):
            move(u, sid).wait_recv()

    def gram(c):
        def body(step, carry):
            j4 = CROWS * c + 4 * step
            rows = jnp.concatenate([
                jnp.concatenate([bmat[pl.ds(j4 + p, ALL, stride=STEP), :],
                                 own[pl.ds(8 * PITCH + PAD + j4 + p, NL, stride=PITCH), :]], axis=0)
                for p in range(4)], axis=1)
            high, low = split(rows)
            a = jnp.concatenate([high, low], axis=0)
            b = jnp.concatenate([high[:ALL], low[:ALL]], axis=0)
            acc[...] += lax.dot_general(a, b, (((1,), (1,)), ((), ())), preferred_element_type=F32)
            return carry

        lax.fori_loop(0, CROWS // 4, body, 0)

    start_own(0)
    start_own(1)
    for copy in local_copies:
        copy.wait()

    @pl.loop(0, 41)
    def _(o):
        own3[o, pl.ds(0, PAD), :] = jnp.zeros((PAD, 128), F32)
        own3[o, pl.ds(PAD + ROWS, 8), :] = jnp.zeros((8, 128), F32)

    @pl.when(space == 0)
    def _():
        left3[...] = jnp.zeros(left3.shape, F32)

    @pl.when(space == 15)
    def _():
        right3[...] = jnp.zeros(right3.shape, F32)

    acc[...] = jnp.zeros(acc.shape, F32)

    def later(g):
        halo_wait((2 * g, 2 * g + 1))
        stencil(own, left, right, pot, g, (hacc, (g - 1) * (8 * STEP)))

    def step(t):
        if t < UNITS:
            forward(t)
        if 1 <= t:
            across(t - 1)
        if t + 2 < UNITS:
            start_own(t + 2)
        halo_start(HALOS.get(t, ()))
        pass_on(PASSES.get(t, ()))

    for t in range(CHUNKS - 2):
        step(t)
        if t >= 2:
            arrived(t - 2)
            gram(t - 2)
        if t == CHUNKS - 3:
            halo_wait((0, 1))
            stencil(own, left, right, pot, 0, (hown2, 0))
            keep = pltpu.make_async_copy(hown.at[:, :, pl.ds(0, ROWS), :], gath.at[1, :, pl.ds(4 * band, 4), pl.ds(0, ROWS), :],
                                         loc_sem.at[4])
            keep.start()
    for t in range(CHUNKS - 2, CHUNKS + 2):
        step(t)
        if t == CHUNKS:
            later(1)
        arrived(t - 2)
        gram(t - 2)

    low64 = lanes((48, 128)) < 64
    both = acc[:96] + acc[96:]
    both = both + pltpu.roll(both, 64, 1)
    gs[...] = jnp.where(low64, both[:48], both[48:])

    def scatter(k):
        return pltpu.make_async_remote_copy(
            src_ref=gs, dst_ref=rbuf.at[turn], send_sem=rs_send.at[k], recv_sem=rs_recv.at[k],
            device_id={"space": half + lax.rem(turn + k, 8)}, device_id_type=MESH)

    cross = pltpu.make_async_remote_copy(
        src_ref=red, dst_ref=full, send_sem=bc_send.at[0], recv_sem=bc_recv.at[0],
        device_id={"space": opposite}, device_id_type=MESH)

    for k in range(1, 8):
        scatter(k).start()
    rbuf[pl.ds(turn, 1)] = gs[...][None]
    later(2)
    step(CHUNKS + 2)
    for k in range(1, 8):
        scatter(k).wait_recv()
    red[...] = jnp.sum(rbuf[...], axis=0)
    cross.start()
    later(3)
    step(CHUNKS + 3)
    cross.wait_recv()

    cells = 16.0 * ROWS * 128
    total = red[...] + full[...]
    total = jnp.concatenate([total, pltpu.roll(total, 64, 1), jnp.zeros((32, 128), F32)], axis=0)
    m1[...] = jnp.transpose(total)[:ALL] * (1.0 / cells)
    lane64 = lanes((ALL, 128))
    row64 = lax.broadcasted_iota(jnp.int32, (ALL, 128), 0)
    m2[...] = jnp.where((lane64 == row64) | (lane64 == row64 + ALL), 1.0, 0.0).astype(F32)
    lane1 = lanes((1, 128))

    def eliminate(k, carry):
        one, two = m1[pl.ds(k, 1), :], m2[pl.ds(k, 1), :]
        pivot = jnp.sum(jnp.where(lane1 == k, one, 0.0), axis=1, keepdims=True)
        whole = m1[...]
        column = jnp.sum(jnp.where(lane64 == k, whole, 0.0), axis=1, keepdims=True)
        factor = jnp.where(row64[:, :1] > k, column / pivot, 0.0)
        m1[...] = whole - factor * one
        m2[...] = m2[...] - factor * two
        return carry

    lax.fori_loop(0, 32, eliminate, 0)
    step(CHUNKS + 4)
    lax.fori_loop(32, 64, eliminate, 0)
    diag = jnp.sum(jnp.where(lane64 == row64, m1[...], 0.0), axis=1, keepdims=True)
    scale = 1.0 / jnp.sqrt(diag)
    tri = m2[...] * scale
    proj = lax.dot_general(m1[...] * scale, tri, (((0,), (0,)), ((), ())),
                           precision=lax.Precision.HIGHEST, preferred_element_type=F32)
    row8 = lax.broadcasted_iota(jnp.int32, (8, ALL), 0)
    wanted = jnp.where(row8 < 4, row8, row8 + 28) + 4 * band
    pick = jnp.where(lanes((8, ALL)) == wanted, 1.0, 0.0).astype(F32)
    mine = jnp.dot(pick, tri, precision=lax.Precision.HIGHEST, preferred_element_type=F32)
    coef = jnp.concatenate([mine, -proj[64:96], jnp.zeros((8, 128), F32)], axis=0)
    high = coef.astype(BF16).astype(F32)
    mixed = jnp.where(lanes((48, 128)) < 64, high, coef - high).astype(BF16)
    lhs[...] = jnp.concatenate([mixed, mixed], axis=1)[:, :192]
    step(CHUNKS + 5)
    later(4)
    step(CHUNKS + 6)
    keep.wait()

    outs = []
    for c in range(CHUNKS):
        arrived(CHUNKS + c)

        def body(step, carry, c=c):
            j4 = CROWS * c + 4 * step
            rows = jnp.concatenate([hmat[pl.ds(j4 + p, ALL, stride=STEP), :] for p in range(4)], axis=1)
            high, low = split(rows)
            rhs = jnp.concatenate([high, high, low], axis=0)
            res = jnp.dot(lhs[...], rhs, preferred_element_type=F32)
            for p in range(4):
                piece = res[:, 128 * p:128 * p + 128]
                oblk2[pl.ds(j4 + p, 8, stride=STEP), :] = piece[:8]
                for g in range(4):
                    where = pl.ds(g * (8 * STEP) + j4 + p, 8, stride=STEP)
                    hacc[where, :] = hacc[where, :] + piece[8 + 8 * g:16 + 8 * g]
            return carry

        lax.fori_loop(0, CROWS // 4, body, 0)
        span = pl.ds(CROWS * c, CROWS)
        outs.append(pltpu.make_async_copy(oblk.at[:, :, span, :], hb_out.at[:, :, span, :], out_sem.at[0, c]))
        outs.append(pltpu.make_async_copy(hacc3.at[:, span, :], hl_out.at[:, span, :], out_sem.at[1, c]))
        outs[-2].start()
        outs[-1].start()

    halo_sent(range(10))
    passed(VIA)
    for u in range(UNITS):
        for sid in range(7):
            move(u, sid).wait_send()
    for k in range(1, 8):
        scatter(k).wait_send()
    cross.wait_send()
    for copy in outs:
        copy.wait()


def hand_over(hb, hl, hb_out, hl_out, held, get, put):
    pairs = [(hb.at[i], hb_out.at[i]) for i in range(2)]
    pairs += [(hl.at[pl.ds(4 * i, 4)], hl_out.at[pl.ds(4 * i, 4)]) for i in range(NL // 4)]
    there = [pltpu.make_async_copy(src, held.at[i], get.at[i]) for i, (src, _) in enumerate(pairs)]
    back = [pltpu.make_async_copy(held.at[i], dst, put.at[i]) for i, (_, dst) in enumerate(pairs)]
    for copy in there:
        copy.start()
    for first, second in zip(there, back):
        first.wait()
        second.start()
    for copy in back:
        copy.wait()


def rows_of(x):
    lead = x.shape[:-2]
    x = x.reshape(*lead, 4, 48, 128)
    return jnp.swapaxes(x, -3, -2).reshape(*lead, ROWS, 128)


def planes_of(x):
    lead = x.shape[:-2]
    x = jnp.swapaxes(x.reshape(*lead, 48, 4, 128), -3, -2)
    return x.reshape(*lead, 4, 48 * 128)


def local(blocks, later, potential):
    hb, hl = pl.pallas_call(
        kernel,
        out_shape=[jax.ShapeDtypeStruct((2, 4, ROWS, 128), F32), jax.ShapeDtypeStruct((NL, ROWS, 128), F32)],
        in_specs=[pl.BlockSpec(memory_space=pl.ANY), pl.BlockSpec(memory_space=pl.ANY),
                  pl.BlockSpec(memory_space=pltpu.VMEM)],
        out_specs=[pl.BlockSpec(memory_space=pl.ANY), pl.BlockSpec(memory_space=pl.ANY)],
        scratch_shapes=[
            pltpu.VMEM((2, 2, 32, STEP, 128), F32),
            pltpu.VMEM((41, PITCH, 128), F32),
            pltpu.VMEM((40, STEP, 128), F32),
            pltpu.VMEM((40, STEP, 128), F32),
            pltpu.VMEM((len(VIA), 4, ROWS, 128), F32),
            pltpu.VMEM((2, 4, STEP, 128), F32),
            pltpu.VMEM((NL, STEP, 128), F32),
            pltpu.VMEM((2, 4, STEP, 128), F32),
            pltpu.VMEM((192, 128), F32),
            pltpu.VMEM((48, 128), F32),
            pltpu.VMEM((8, 48, 128), F32),
            pltpu.VMEM((48, 128), F32),
            pltpu.VMEM((48, 128), F32),
            pltpu.VMEM((ALL, 128), F32),
            pltpu.VMEM((ALL, 128), F32),
            pltpu.VMEM((48, 192), BF16),
            pltpu.SemaphoreType.DMA((5,)),
            pltpu.SemaphoreType.DMA((UNITS, 7)),
            pltpu.SemaphoreType.DMA((UNITS, 7)),
            pltpu.SemaphoreType.DMA((10, 2)),
            pltpu.SemaphoreType.DMA((10, 2)),
            pltpu.SemaphoreType.DMA((len(VIA),)),
            pltpu.SemaphoreType.DMA((len(VIA),)),
            pltpu.SemaphoreType.DMA((8,)),
            pltpu.SemaphoreType.DMA((8,)),
            pltpu.SemaphoreType.DMA((1,)),
            pltpu.SemaphoreType.DMA((1,)),
            pltpu.SemaphoreType.DMA((2, CHUNKS)),
        ],
        compiler_params=pltpu.CompilerParams(
            collective_id=0, has_side_effects=True, vmem_limit_bytes=56 * 1024 * 1024),
    )(rows_of(blocks), rows_of(later), rows_of(potential))
    count = 2 + NL // 4
    hb, hl = pl.pallas_call(
        hand_over,
        out_shape=[jax.ShapeDtypeStruct(hb.shape, F32), jax.ShapeDtypeStruct(hl.shape, F32)],
        in_specs=[pl.BlockSpec(memory_space=pl.ANY)] * 2,
        out_specs=[pl.BlockSpec(memory_space=pl.ANY)] * 2,
        scratch_shapes=[pltpu.VMEM((count, 4, ROWS, 128), F32), pltpu.SemaphoreType.DMA((count,)),
                        pltpu.SemaphoreType.DMA((count,))],
        compiler_params=pltpu.CompilerParams(vmem_limit_bytes=56 * 1024 * 1024),
    )(hb, hl)
    return planes_of(hb), planes_of(hl)


def solution(mesh):
    return jax.shard_map(
        local,
        mesh=mesh,
        in_specs=(P(None, "band", "space", None), P("band", "space", None), P("space", None)),
        out_specs=(P(None, "band", "space", None), P("band", "space", None)),
        check_vma=False,
    )
```

```python
import functools

import jax
import jax.numpy as jnp
from jax import lax
from jax.experimental import pallas as pl
from jax.experimental.pallas import tpu as pltpu
from jax.sharding import PartitionSpec as P

MESH = pl.DeviceIdType.MESH
F32 = jnp.float32
BF16 = jnp.bfloat16
NZ = 96
ROWS = 192
PAD = 16
PITCH = 216
STEP = 200
CHUNKS = 6
CROWS = ROWS // CHUNKS
UNITS = 2 * CHUNKS
HALOS = {0: (0, 3), 1: (1,), 2: (2, 5), 4: (4, 7), 6: (6, 9), 8: (8,)}
PASSES = {2: (3,), 4: (5,), 6: (7,), 8: (9,)}
NB = 8
NL = 32
VIA = (3, 5, 7, 9)
ALL = 64
weights = (-205.0 / 72.0, 8.0 / 5.0, -1.0 / 5.0, 8.0 / 315.0, -1.0 / 560.0)


def lanes(shape=(8, 128)):
    return lax.broadcasted_iota(jnp.int32, shape, len(shape) - 1)


def split(value):
    high = value.astype(BF16)
    return high, (value - high.astype(F32)).astype(BF16)


def stencil(own, left, right, pot, group, out):
    ref, base = out
    lane = lanes()

    def load(chunk, plane):
        return own[pl.ds(group * (8 * PITCH) + PAD + 4 * chunk + plane, 8, stride=PITCH), :]

    def shifted(row, shift):
        q, e = shift // 128, shift % 128
        if e == 0:
            return row[q + 3]
        mixed = jnp.where(lane >= e, row[q + 3], row[q + 4])
        return pltpu.roll(mixed, 128 - e, 1)

    def one(chunk, third):
        zpos = lane + 32 * third
        zpos = jnp.where(zpos >= NZ, zpos - NZ, zpos)
        rows = [[load(chunk + d, plane) for d in range(-3, 4)] for plane in range(4)]
        halo = group * (8 * STEP) + 4 * chunk
        xs = [left[pl.ds(halo + plane, 8, stride=STEP), :] for plane in range(4)]
        xs += [rows[plane][3] for plane in range(4)]
        xs += [right[pl.ds(halo + plane, 8, stride=STEP), :] for plane in range(4)]
        for plane in range(4):
            row = rows[plane]
            acc = (pot[pl.ds(4 * chunk + plane, 1), :] - 1.5 * weights[0]) * row[3]
            for k in range(1, 5):
                part = xs[4 + plane + k] + xs[4 + plane - k]
                part = part + (shifted(row, NZ * k) + shifted(row, -NZ * k))
                up = jnp.where(zpos < NZ - k, shifted(row, k), 0.0)
                down = jnp.where(zpos >= k, shifted(row, -k), 0.0)
                acc = acc + (-0.5 * weights[k]) * (part + (up + down))
            ref[pl.ds(base + 4 * chunk + plane, 8, stride=STEP), :] = acc

    def body(step, carry):
        for third in range(3):
            one(3 * step + third, third)
        return carry

    lax.fori_loop(0, ROWS // 12, body, 0)


def kernel(blk, lat, pot, hb_out, hl_out,
           gath, own3, left3, right3, relay, hown, hacc3, oblk,
           acc, gs, rbuf, red, full, m1, m2, lhs,
           loc_sem, ag_send, ag_recv, halo_send, halo_recv, relay_send, relay_recv, rs_send, rs_recv, bc_send, bc_recv, out_sem):
    space = lax.axis_index("space")
    band = lax.axis_index("band")
    z, y = band // 4, band % 4

    def at(dy, dz):
        return lax.rem(z + dz, 2) * 4 + lax.rem(y + dy + 4, 4)

    own = own3.reshape(41 * PITCH, 128)
    left = left3.reshape(40 * STEP, 128)
    right = right3.reshape(40 * STEP, 128)
    hacc = hacc3.reshape(NL * STEP, 128)
    hown2 = hown.reshape(NB * STEP, 128)
    oblk2 = oblk.reshape(NB * STEP, 128)
    bmat = gath.at[0].reshape(ALL * STEP, 128)
    hmat = gath.at[1].reshape(ALL * STEP, 128)

    barrier = pltpu.get_barrier_semaphore()
    for b in (at(1, 0), at(-1, 0), at(0, 1)):
        pl.semaphore_signal(barrier, inc=1, device_id={"band": b}, device_id_type=MESH)

    half = space // 8 * 8
    turn = space - half

    @pl.loop(1, 8)
    def _(k):
        pl.semaphore_signal(barrier, inc=1, device_id={"space": half + lax.rem(turn + k, 8)}, device_id_type=MESH)

    opposite = lax.rem(space + 8, 16)
    pl.semaphore_signal(barrier, inc=1, device_id={"space": opposite}, device_id_type=MESH)
    pl.semaphore_signal(barrier, inc=1, device_id={"space": 15 - space}, device_id_type=MESH)

    local_copies = [
        pltpu.make_async_copy(blk.at[0], own3.at[pl.ds(0, 4), pl.ds(PAD, ROWS), :], loc_sem.at[0]),
        pltpu.make_async_copy(blk.at[1], own3.at[pl.ds(4, 4), pl.ds(PAD, ROWS), :], loc_sem.at[1]),
        pltpu.make_async_copy(lat, own3.at[pl.ds(8, NL), pl.ds(PAD, ROWS), :], loc_sem.at[2]),
        pltpu.make_async_copy(blk, gath.at[0, :, pl.ds(4 * band, 4), pl.ds(0, ROWS), :], loc_sem.at[3]),
    ]
    for copy in local_copies:
        copy.start()
    pl.semaphore_wait(barrier, 12)

    def source(part):
        return blk.at[part] if part < 2 else lat.at[pl.ds(4 * (part - 2), 4)]

    def halo(part, side):
        ref = left3 if side == 0 else right3
        return pltpu.make_async_remote_copy(
            src_ref=source(part), dst_ref=ref.at[pl.ds(4 * part, 4), pl.ds(0, ROWS), :],
            send_sem=halo_send.at[part, side], recv_sem=halo_recv.at[part, side],
            device_id={"space": space + 1 if side == 0 else space - 1}, device_id_type=MESH)

    def detour(part, side):
        return pltpu.make_async_remote_copy(
            src_ref=source(part), dst_ref=relay.at[VIA.index(part)],
            send_sem=halo_send.at[part, side], recv_sem=relay_recv.at[VIA.index(part)],
            device_id={"space": space + 8 if side == 0 else space - 8}, device_id_type=MESH)

    def onward(part, side):
        ref = left3 if side == 0 else right3
        return pltpu.make_async_remote_copy(
            src_ref=relay.at[VIA.index(part)], dst_ref=ref.at[pl.ds(4 * part, 4), pl.ds(0, ROWS), :],
            send_sem=relay_send.at[VIA.index(part)], recv_sem=halo_recv.at[part, side],
            device_id={"space": space - 7 if side == 0 else space + 7}, device_id_type=MESH)

    senders = ((space < 15, space == 7, space != 7), (space > 0, space == 8, space != 8))

    def halo_each(parts, direct, around):
        for side, (any_, seam, inner) in enumerate(senders):
            @pl.when(any_)
            def _(side=side):
                for part in parts:
                    if part not in VIA:
                        direct(part, side)

            if set(VIA) & set(parts):
                @pl.when(any_ & inner)
                def _(side=side):
                    for part in parts:
                        if part in VIA:
                            direct(part, side)

                @pl.when(seam)
                def _(side=side):
                    for part in parts:
                        if part in VIA:
                            around(part, side)

    def halo_start(parts):
        halo_each(parts, lambda p, s: halo(p, s).start(), lambda p, s: detour(p, s).start())

    def halo_sent(parts):
        halo_each(parts, lambda p, s: halo(p, s).wait_send(), lambda p, s: detour(p, s).wait_send())

    def halo_wait(parts):
        for side, there in enumerate((space > 0, space < 15)):
            @pl.when(there)
            def _(side=side):
                for part in parts:
                    halo(part, side).wait_recv()

    def pass_on(parts):
        for side, here in enumerate((space == 15, space == 0)):
            @pl.when(here)
            def _(side=side):
                for part in parts:
                    detour(part, side).wait_recv()
                    onward(part, side).start()

    def passed(parts):
        for side, here in enumerate((space == 15, space == 0)):
            @pl.when(here)
            def _(side=side):
                for part in parts:
                    onward(part, side).wait_send()

    def slot(u, b):
        return gath.at[u // CHUNKS, :, pl.ds(4 * b, 4), pl.ds(CROWS * (u % CHUNKS), CROWS), :]

    def move(u, sid):
        even = u % 2 == 0
        source, to = {
            0: ((0, 0), (1, 0)), 1: ((0, 0), (-1, 0)), 2: ((0, 0), (0, 1)),
            3: ((-1, 0), (1, 0)) if even else ((1, 0), (-1, 0)),
            4: ((0, 1), (1, 0)), 5: ((0, 1), (-1, 0)), 6: ((2, 0), (0, 1)),
        }[sid]
        place = slot(u, at(*source))
        if sid < 3:
            part = blk if u < CHUNKS else hown
            src = part.at[:, :, pl.ds(CROWS * (u % CHUNKS), CROWS), :]
        else:
            src = place
        return pltpu.make_async_remote_copy(
            src_ref=src, dst_ref=place, send_sem=ag_send.at[u, sid], recv_sem=ag_recv.at[u, sid],
            device_id={"band": at(*to)}, device_id_type=MESH)

    def start_own(u):
        for sid in (0, 1, 2):
            move(u, sid).start()

    def forward(u):
        move(u, 0 if u % 2 == 0 else 1).wait_recv()
        move(u, 3).start()
        move(u, 2).wait_recv()
        move(u, 4).start()
        move(u, 5).start()

    def across(u):
        move(u, 3).wait_recv()
        move(u, 6).start()

    def arrived(u):
        for sid in (1 if u % 2 == 0 else 0, 4, 5, 6):
            move(u, sid).wait_recv()

    def gram(c):
        def body(step, carry):
            j4 = CROWS * c + 4 * step
            rows = jnp.concatenate([
                jnp.concatenate([bmat[pl.ds(j4 + p, ALL, stride=STEP), :],
                                 own[pl.ds(8 * PITCH + PAD + j4 + p, NL, stride=PITCH), :]], axis=0)
                for p in range(4)], axis=1)
            high, low = split(rows)
            a = jnp.concatenate([high, low], axis=0)
            b = jnp.concatenate([high[:ALL], low[:ALL]], axis=0)
            acc[...] += lax.dot_general(a, b, (((1,), (1,)), ((), ())), preferred_element_type=F32)
            return carry

        lax.fori_loop(0, CROWS // 4, body, 0)

    start_own(0)
    start_own(1)
    for copy in local_copies:
        copy.wait()

    @pl.loop(0, 41)
    def _(o):
        own3[o, pl.ds(0, PAD), :] = jnp.zeros((PAD, 128), F32)
        own3[o, pl.ds(PAD + ROWS, 8), :] = jnp.zeros((8, 128), F32)

    @pl.when(space == 0)
    def _():
        left3[...] = jnp.zeros(left3.shape, F32)

    @pl.when(space == 15)
    def _():
        right3[...] = jnp.zeros(right3.shape, F32)

    acc[...] = jnp.zeros(acc.shape, F32)

    def later(g):
        halo_wait((2 * g, 2 * g + 1))
        stencil(own, left, right, pot, g, (hacc, (g - 1) * (8 * STEP)))

    def sent(u):
        for sid in range(7):
            move(u, sid).wait_send()

    def step(t):
        if t < UNITS:
            forward(t)
        if 1 <= t:
            across(t - 1)
        if t + 2 < UNITS:
            start_own(t + 2)
        if t >= 4:
            sent(t - 4)
        halo_start(HALOS.get(t, ()))
        pass_on(PASSES.get(t, ()))

    for t in range(CHUNKS - 2):
        step(t)
        if t >= 2:
            arrived(t - 2)
            gram(t - 2)
        if t == CHUNKS - 3:
            halo_wait((0, 1))
            stencil(own, left, right, pot, 0, (hown2, 0))
            keep = pltpu.make_async_copy(hown.at[:, :, pl.ds(0, ROWS), :], gath.at[1, :, pl.ds(4 * band, 4), pl.ds(0, ROWS), :],
                                         loc_sem.at[4])
            keep.start()
    for t in range(CHUNKS - 2, CHUNKS + 2):
        step(t)
        if t == CHUNKS:
            later(1)
        arrived(t - 2)
        gram(t - 2)

    low64 = lanes((48, 128)) < 64
    both = acc[:96] + acc[96:]
    both = both + pltpu.roll(both, 64, 1)
    gs[...] = jnp.where(low64, both[:48], both[48:])

    def scatter(k):
        return pltpu.make_async_remote_copy(
            src_ref=gs, dst_ref=rbuf.at[turn], send_sem=rs_send.at[k], recv_sem=rs_recv.at[k],
            device_id={"space": half + lax.rem(turn + k, 8)}, device_id_type=MESH)

    cross = pltpu.make_async_remote_copy(
        src_ref=red, dst_ref=full, send_sem=bc_send.at[0], recv_sem=bc_recv.at[0],
        device_id={"space": opposite}, device_id_type=MESH)

    for k in range(1, 8):
        scatter(k).start()
    rbuf[pl.ds(turn, 1)] = gs[...][None]
    later(2)
    step(CHUNKS + 2)
    for k in range(1, 8):
        scatter(k).wait_recv()
    red[...] = jnp.sum(rbuf[...], axis=0)
    cross.start()
    later(3)
    step(CHUNKS + 3)
    cross.wait_recv()

    cells = 16.0 * ROWS * 128
    total = red[...] + full[...]
    total = jnp.concatenate([total, pltpu.roll(total, 64, 1), jnp.zeros((32, 128), F32)], axis=0)
    m1[...] = jnp.transpose(total)[:ALL] * (1.0 / cells)
    lane64 = lanes((ALL, 128))
    row64 = lax.broadcasted_iota(jnp.int32, (ALL, 128), 0)
    m2[...] = jnp.where((lane64 == row64) | (lane64 == row64 + ALL), 1.0, 0.0).astype(F32)
    lane1 = lanes((1, 128))

    def eliminate(k, carry):
        one, two = m1[pl.ds(k, 1), :], m2[pl.ds(k, 1), :]
        pivot = jnp.sum(jnp.where(lane1 == k, one, 0.0), axis=1, keepdims=True)
        whole = m1[...]
        column = jnp.sum(jnp.where(lane64 == k, whole, 0.0), axis=1, keepdims=True)
        factor = jnp.where(row64[:, :1] > k, column / pivot, 0.0)
        m1[...] = whole - factor * one
        m2[...] = m2[...] - factor * two
        return carry

    lax.fori_loop(0, 32, eliminate, 0)
    step(CHUNKS + 4)
    lax.fori_loop(32, 64, eliminate, 0)
    diag = jnp.sum(jnp.where(lane64 == row64, m1[...], 0.0), axis=1, keepdims=True)
    scale = 1.0 / jnp.sqrt(diag)
    tri = m2[...] * scale
    proj = lax.dot_general(m1[...] * scale, tri, (((0,), (0,)), ((), ())),
                           precision=lax.Precision.HIGHEST, preferred_element_type=F32)
    row8 = lax.broadcasted_iota(jnp.int32, (8, ALL), 0)
    wanted = jnp.where(row8 < 4, row8, row8 + 28) + 4 * band
    pick = jnp.where(lanes((8, ALL)) == wanted, 1.0, 0.0).astype(F32)
    mine = jnp.dot(pick, tri, precision=lax.Precision.HIGHEST, preferred_element_type=F32)
    coef = jnp.concatenate([mine, -proj[64:96], jnp.zeros((8, 128), F32)], axis=0)
    high = coef.astype(BF16).astype(F32)
    mixed = jnp.where(lanes((48, 128)) < 64, high, coef - high).astype(BF16)
    lhs[...] = jnp.concatenate([mixed, mixed], axis=1)[:, :192]
    step(CHUNKS + 5)
    later(4)
    step(CHUNKS + 6)
    keep.wait()

    outs = []
    for c in range(CHUNKS):
        arrived(CHUNKS + c)

        def body(step, carry, c=c):
            j4 = CROWS * c + 4 * step
            rows = jnp.concatenate([hmat[pl.ds(j4 + p, ALL, stride=STEP), :] for p in range(4)], axis=1)
            high, low = split(rows)
            rhs = jnp.concatenate([high, high, low], axis=0)
            res = jnp.dot(lhs[...], rhs, preferred_element_type=F32)
            for p in range(4):
                piece = res[:, 128 * p:128 * p + 128]
                oblk2[pl.ds(j4 + p, 8, stride=STEP), :] = piece[:8]
                for g in range(4):
                    where = pl.ds(g * (8 * STEP) + j4 + p, 8, stride=STEP)
                    hacc[where, :] = hacc[where, :] + piece[8 + 8 * g:16 + 8 * g]
            return carry

        lax.fori_loop(0, CROWS // 4, body, 0)
        span = pl.ds(CROWS * c, CROWS)
        outs.append(pltpu.make_async_copy(oblk.at[:, :, span, :], hb_out.at[:, :, span, :], out_sem.at[0, c]))
        outs.append(pltpu.make_async_copy(hacc3.at[:, span, :], hl_out.at[:, span, :], out_sem.at[1, c]))
        outs[-2].start()
        outs[-1].start()

    halo_sent(range(10))
    passed(VIA)
    for u in range(UNITS - 3, UNITS):
        sent(u)
    for k in range(1, 8):
        scatter(k).wait_send()
    cross.wait_send()
    for copy in outs:
        copy.wait()


def hand_over(hb, hl, hb_out, hl_out, held, get, put):
    pairs = [(hb.at[i], hb_out.at[i]) for i in range(2)]
    pairs += [(hl.at[pl.ds(4 * i, 4)], hl_out.at[pl.ds(4 * i, 4)]) for i in range(NL // 4)]
    there = [pltpu.make_async_copy(src, held.at[i], get.at[i]) for i, (src, _) in enumerate(pairs)]
    back = [pltpu.make_async_copy(held.at[i], dst, put.at[i]) for i, (_, dst) in enumerate(pairs)]
    for copy in there:
        copy.start()
    for first, second in zip(there, back):
        first.wait()
        second.start()
    for copy in back:
        copy.wait()


def rows_of(x):
    lead = x.shape[:-2]
    x = x.reshape(*lead, 4, 48, 128)
    return jnp.swapaxes(x, -3, -2).reshape(*lead, ROWS, 128)


def planes_of(x):
    lead = x.shape[:-2]
    x = jnp.swapaxes(x.reshape(*lead, 48, 4, 128), -3, -2)
    return x.reshape(*lead, 4, 48 * 128)


def local(blocks, later, potential):
    hb, hl = pl.pallas_call(
        kernel,
        out_shape=[jax.ShapeDtypeStruct((2, 4, ROWS, 128), F32), jax.ShapeDtypeStruct((NL, ROWS, 128), F32)],
        in_specs=[pl.BlockSpec(memory_space=pl.ANY), pl.BlockSpec(memory_space=pl.ANY),
                  pl.BlockSpec(memory_space=pltpu.VMEM)],
        out_specs=[pl.BlockSpec(memory_space=pl.ANY), pl.BlockSpec(memory_space=pl.ANY)],
        scratch_shapes=[
            pltpu.VMEM((2, 2, 32, STEP, 128), F32),
            pltpu.VMEM((41, PITCH, 128), F32),
            pltpu.VMEM((40, STEP, 128), F32),
            pltpu.VMEM((40, STEP, 128), F32),
            pltpu.VMEM((len(VIA), 4, ROWS, 128), F32),
            pltpu.VMEM((2, 4, STEP, 128), F32),
            pltpu.VMEM((NL, STEP, 128), F32),
            pltpu.VMEM((2, 4, STEP, 128), F32),
            pltpu.VMEM((192, 128), F32),
            pltpu.VMEM((48, 128), F32),
            pltpu.VMEM((8, 48, 128), F32),
            pltpu.VMEM((48, 128), F32),
            pltpu.VMEM((48, 128), F32),
            pltpu.VMEM((ALL, 128), F32),
            pltpu.VMEM((ALL, 128), F32),
            pltpu.VMEM((48, 192), BF16),
            pltpu.SemaphoreType.DMA((5,)),
            pltpu.SemaphoreType.DMA((UNITS, 7)),
            pltpu.SemaphoreType.DMA((UNITS, 7)),
            pltpu.SemaphoreType.DMA((10, 2)),
            pltpu.SemaphoreType.DMA((10, 2)),
            pltpu.SemaphoreType.DMA((len(VIA),)),
            pltpu.SemaphoreType.DMA((len(VIA),)),
            pltpu.SemaphoreType.DMA((8,)),
            pltpu.SemaphoreType.DMA((8,)),
            pltpu.SemaphoreType.DMA((1,)),
            pltpu.SemaphoreType.DMA((1,)),
            pltpu.SemaphoreType.DMA((2, CHUNKS)),
        ],
        compiler_params=pltpu.CompilerParams(
            collective_id=0, has_side_effects=True, vmem_limit_bytes=56 * 1024 * 1024),
    )(rows_of(blocks), rows_of(later), rows_of(potential))
    count = 2 + NL // 4
    hb, hl = pl.pallas_call(
        hand_over,
        out_shape=[jax.ShapeDtypeStruct(hb.shape, F32), jax.ShapeDtypeStruct(hl.shape, F32)],
        in_specs=[pl.BlockSpec(memory_space=pl.ANY)] * 2,
        out_specs=[pl.BlockSpec(memory_space=pl.ANY)] * 2,
        scratch_shapes=[pltpu.VMEM((count, 4, ROWS, 128), F32), pltpu.SemaphoreType.DMA((count,)),
                        pltpu.SemaphoreType.DMA((count,))],
        compiler_params=pltpu.CompilerParams(vmem_limit_bytes=56 * 1024 * 1024),
    )(hb, hl)
    return planes_of(hb), planes_of(hl)


def solution(mesh):
    return jax.shard_map(
        local,
        mesh=mesh,
        in_specs=(P(None, "band", "space", None), P("band", "space", None), P("space", None)),
        out_specs=(P(None, "band", "space", None), P("band", "space", None)),
        check_vma=False,
    )
```
